1024 devices in a mesh: row: 32 (over y, z_lo, core), col: 32 (over z_hi, x).
Axes of the slice: x: 8, y: 8, z: 8 (z_hi: 4, z_lo: 2; z = z_hi * 2 + z_lo), core: 2. Of those that a mesh axis runs over, the one named last changes fastest.
Arguments:
- objects: float32 [2, 2, 8192, 8192], P(None, None, 'row', 'col'), may hold values from -5 to 5
- probe: float32 [2, 2, 128, 128], replicated, may hold values from -6 to 6
- amplitudes: bfloat16 [32, 32, 6, 128, 128], P('row', 'col'), may hold values from 0.29882812 to 3
- owners: int32 [32, 32, 6], P('row', 'col'), may hold values from 0 to 31, as said below
- off_rows: int32 [32, 32, 6], P('row', 'col'), may hold values from 0 to 256
- off_cols: int32 [32, 32, 6], P('row', 'col'), may hold values from 0 to 256
Outputs:
- gradient: float32 [2, 2, 8192, 8192], P(None, None, 'row', 'col')
The draws below stay inside these ranges and needn't reach their ends.
Inputs may be any that keep to these rules, and one draw needn't show every extreme that they name: Each device's 6 positions go to owners of its own tile row whose tile column is the device's own plus one of -3, -2, -1, 1, 2, 3, 4, taken modulo 32; at most 2 of them to one owner, exactly 2 to one owner from some device of every tile row. Over all devices of a tile row, one owner receives exactly 12 positions and every other owner at most 7.
All inputs are finite; a program needn't handle non-finite values.
Results may differ from the reference program's by a relative error of at most 0.009.
Values may be sent and summed in bfloat16 or wider, within the bound.
A program may use at most 32 MiB of HBM per device.

```python
import math
import jax
import jax.numpy as jnp
from jax import lax

P_SIZE = 128
MODES = 2
SLICES = 2
SRC_DEV = 6
TH = 256
TW = 256
B = 64
GRID_R = 32
GRID_C = 32
OH = 8192
OW = 8192


REACH_OFFSETS = (-3, -2, -1, 1, 2, 3, 4)


def draw_owners(key, part):
    keys = jax.random.split(key, GRID_R)
    reach = jnp.array(REACH_OFFSETS, dtype=jnp.int32)
    kinds = reach.shape[0]

    def one_row(row_key):
        first, second, third, fourth = jax.random.split(row_key, 4)
        hottest = jax.random.randint(first, (), 0, GRID_C, dtype=jnp.int32)
        hot_order = jax.random.permutation(second, kinds).astype(jnp.int32)
        cold_kind = hot_order[kinds - 1]
        sources = jnp.arange(GRID_C, dtype=jnp.int32)
        apart = (hottest - sources) % GRID_C
        match = apart[:, None] == reach[None, :] % GRID_C
        kind_ids = jnp.arange(kinds, dtype=jnp.int32)
        is_cold = kind_ids[None, :] == cold_kind
        hot_match = match & jnp.logical_not(is_cold)
        cold_match = match & is_cold
        hot_source = jnp.any(hot_match, axis=1)
        raw = jax.random.randint(third, (GRID_C, kinds), 0, 1000, dtype=jnp.int32)
        scores = raw * 8 + kind_ids[None, :]
        scores = jnp.where(hot_match, -1, jnp.where(cold_match, 100000, scores))
        order = jnp.argsort(scores, axis=1, stable=True)[:, :SRC_DEV]
        base = (sources[:, None] + reach[order]) % GRID_C
        slot = jnp.arange(SRC_DEV, dtype=jnp.int32)
        moved = hot_source[:, None] & (slot[None, :] == 1)
        owners_row = jnp.where(moved, hottest, base).astype(jnp.int32)
        mix = jax.random.randint(fourth, (GRID_C, SRC_DEV), 0, 1000, dtype=jnp.int32)
        mix = mix * 8 + slot[None, :]
        shuffle = jnp.argsort(mix, axis=1, stable=True)
        return jnp.take_along_axis(owners_row, shuffle, axis=1).astype(jnp.int32)
    return jax.vmap(one_row)(keys)


def plant(result, own_key, low, top_value):
    longest = result.shape.index(max(result.shape))
    spots = []
    for shift in (0, 1):
        where = [jax.random.randint(jax.random.fold_in(own_key, axis), (), 0, length) for axis, length in enumerate(result.shape)]
        where[longest] = (where[longest] + shift) % result.shape[longest]
        spots.append(tuple(where))
    return result.at[spots[0]].set(low).at[spots[1]].set(top_value)


def steps_of(stream_key, shape, pieces, smallest, high):
    factor_of = 1.0
    for axis_at, parts in pieces:
        steps = jax.random.uniform(jax.random.fold_in(jax.random.fold_in(stream_key, 6), axis_at), (parts,), jnp.float32, smallest / len(pieces), high / len(pieces))
        factor_of = factor_of * jnp.repeat(jnp.exp(steps), shape[axis_at] // parts).reshape((-1,) + (1,) * (len(shape) - 1 - axis_at))
    return factor_of


def gaussian(rng, dims, scale, bound, cuts=(), kind=jnp.bfloat16):
    drawn = scale * jax.random.normal(rng, dims, jnp.float32)
    if cuts:
        drawn = drawn * steps_of(rng, dims, cuts, -0.22, 0.18)
    return jnp.clip(drawn, -bound, bound).astype(kind)


def setup_inputs(seed: int = 0) -> dict:
    key_list = jax.random.split(jax.random.key(seed), 7)
    return {
        "objects": gaussian(key_list[0], (SLICES, 2, OH, OW), 0.7, 5.0, ((2, 32), (3, 32)), jnp.float32),
        "probe": gaussian(key_list[1], (MODES, 2, P_SIZE, P_SIZE), 1.0, 6.0, (), jnp.float32),
        "amplitudes": jnp.clip(jnp.exp(math.log(3.0) - 2.306499 * jax.random.uniform(key_list[2], (GRID_R, GRID_C, SRC_DEV, P_SIZE, P_SIZE), jnp.float32) ** steps_of(key_list[2], (GRID_R, GRID_C, SRC_DEV, P_SIZE, P_SIZE), ((0, 32), (1, 32)), -0.2, 0.2)), 0.29882812, 3.0).astype(jnp.bfloat16),
        "owners": draw_owners(jax.random.fold_in(key_list[6], 71), 0),
        "off_rows": plant(jax.random.randint(key_list[4], (GRID_R, GRID_C, SRC_DEV), 0, TH + 2 * B - P_SIZE + 1), jax.random.fold_in(key_list[4], 1), 0, TH + 2 * B - P_SIZE).astype(jnp.int32),
        "off_cols": plant(jax.random.randint(key_list[5], (GRID_R, GRID_C, SRC_DEV), 0, TW + 2 * B - P_SIZE + 1), jax.random.fold_in(key_list[5], 1), 0, TW + 2 * B - P_SIZE).astype(jnp.int32),
    }


FRESNEL = 24.0

def make_mats(width):
    idx = jnp.arange(width, dtype=jnp.int32)
    prod = idx[:, None] * idx[None, :] % width
    angle = prod.astype(jnp.float32) * (2.0 * math.pi / width)
    scale = 1.0 / math.sqrt(width)
    f_re = jnp.cos(angle) * scale
    f_im = -jnp.sin(angle) * scale
    centred = (idx + width // 2) % width - width // 2
    theta = (centred * centred).astype(jnp.float32) * (math.pi * FRESNEL / (width * width))
    d_re = jnp.cos(theta)
    d_im = -jnp.sin(theta)
    m_re = d_re[:, None] * f_re - d_im[:, None] * f_im
    m_im = d_re[:, None] * f_im + d_im[:, None] * f_re
    high = lax.Precision.HIGHEST
    k_re = jnp.dot(f_re, m_re, precision=high) + jnp.dot(f_im, m_im, precision=high)
    k_im = jnp.dot(f_re, m_im, precision=high) - jnp.dot(f_im, m_re, precision=high)
    f_re = f_re.astype(jnp.bfloat16)
    f_im = f_im.astype(jnp.bfloat16)
    k_re = k_re.astype(jnp.bfloat16)
    k_im = k_im.astype(jnp.bfloat16)

    def left_stack(a_re, a_im):
        return jnp.stack([jnp.stack([a_re, -a_im]), jnp.stack([a_im, a_re])])

    def right_stack(a_re, a_im):
        return jnp.stack([jnp.stack([a_re, a_im]), jnp.stack([-a_im, a_re])])
    return (left_stack(k_re, k_im), right_stack(k_re, k_im), left_stack(f_re, f_im), right_stack(f_re, f_im), left_stack(k_re, -k_im), right_stack(k_re, -k_im), left_stack(f_re, -f_im), right_stack(f_re, -f_im))

def apply_left(table, field):
    return jnp.einsum('trpq,nrqs->ntps', table.astype(jnp.float32), field.astype(jnp.float32))

def apply_right(field, table):
    return jnp.einsum('nrpq,rtqs->ntps', field.astype(jnp.float32), table.astype(jnp.float32))

def cmul(first, second):
    a_re = first[..., 0, :, :]
    a_im = first[..., 1, :, :]
    b_re = second[..., 0, :, :]
    b_im = second[..., 1, :, :]
    return jnp.stack([a_re * b_re - a_im * b_im, a_re * b_im + a_im * b_re], axis=-3)

def conj(field):
    return jnp.stack([field[..., 0, :, :], -field[..., 1, :, :]], axis=-3)

def pattern_grad(window, probe, amp, valid, mats):
    k_left, k_right, f_left, f_right, kc_left, kc_right, fc_left, fc_right = mats
    psi_one = cmul(probe, window[0]).astype(jnp.bfloat16)
    upper = apply_left(k_left, psi_one).astype(jnp.bfloat16)
    phi = apply_right(upper, k_right)
    psi_two = cmul(phi, window[1]).astype(jnp.bfloat16)
    vfield = apply_left(f_left, psi_two).astype(jnp.bfloat16)
    far = apply_right(vfield, f_right)
    inten = lax.optimization_barrier(jnp.sum(far * far, axis=(0, 1)))
    ratio = amp.astype(jnp.float32) / jnp.maximum(jnp.sqrt(inten), 1.0)
    resid = (far * (valid * (1.0 - ratio))).astype(jnp.bfloat16)
    wfield = apply_left(fc_left, resid).astype(jnp.bfloat16)
    g_two = apply_right(wfield, fc_right)
    g_phi = cmul(conj(window[1]), g_two).astype(jnp.bfloat16)
    yfield = apply_left(kc_left, g_phi).astype(jnp.bfloat16)
    g_one = apply_right(yfield, kc_right)
    grad_one = lax.optimization_barrier(jnp.sum(cmul(conj(probe), g_one), axis=0))
    grad_two = lax.optimization_barrier(jnp.sum(cmul(conj(phi), g_two), axis=0))
    return jnp.stack([grad_one, grad_two])

def reference(objects, probe, amplitudes, owners, off_rows, off_cols):
    mats = make_mats(P_SIZE)
    padded = jnp.pad(objects, ((0, 0), (0, 0), (B, B), (B, B)))
    total = GRID_R * GRID_C * SRC_DEV
    row_index = jnp.arange(total, dtype=jnp.int32) // (GRID_C * SRC_DEV)
    amps = amplitudes.reshape(total, P_SIZE, P_SIZE)
    dest = owners.reshape(total).astype(jnp.int32)
    start_rows = (row_index * TH + off_rows.reshape(total)).astype(jnp.int32)
    start_cols = (dest * TW + off_cols.reshape(total)).astype(jnp.int32)

    def visit(carry, item):
        srow, scol, amp = item
        zero = jnp.zeros((), jnp.int32)
        corner = (zero, zero, srow, scol)
        window = lax.dynamic_slice(padded, corner, (SLICES, 2, P_SIZE, P_SIZE))
        grads = pattern_grad(window, probe, amp, 1.0, mats)
        current = lax.dynamic_slice(carry, corner, (SLICES, 2, P_SIZE, P_SIZE))
        return (lax.dynamic_update_slice(carry, current + grads, corner), None)
    start = jnp.zeros(padded.shape, jnp.float32)
    summed, _ = lax.scan(visit, start, (start_rows, start_cols, amps))
    return summed[:, :, B:B + OH, B:B + OW]
```

```python
import functools
import math

import jax
import jax.numpy as jnp
import numpy as np
from jax import lax
from jax.experimental import pallas as pl
from jax.experimental.pallas import tpu as pltpu
from jax.sharding import PartitionSpec as P

MESH = pl.DeviceIdType.MESH
REACH = (-3, -2, -1, 1, 2, 3, 4)
KINDS = len(REACH)
CAP = 2
SLOTS = CAP * KINDS
RMAX = 12
FRESNEL = 24.0
F32 = jnp.float32
BF16 = jnp.bfloat16
N = 128
B = 64
T = 256
EXT = T + 2 * B
CH = 4
SIDES = ((-1, 0), (1, 0), (0, -1), (0, 1), (-1, -1), (-1, 1), (1, -1), (1, 1))
PARTNERS = SIDES + tuple((0, d) for d in (-4, -3, -2, 2, 3, 4))


def tables():
    k = np.arange(N)
    f = np.exp(-2j * np.pi * ((k[:, None] * k[None, :]) % N) / N) / math.sqrt(N)
    c = (k + N // 2) % N - N // 2
    d = np.exp(-1j * np.pi * FRESNEL * c * c / (N * N))
    kk = np.conj(f) @ (d[:, None] * f)

    def left(a):
        a = np.block([[a.real, -a.imag], [a.imag, a.real]]).astype(np.float32)
        return jnp.asarray(a).astype(BF16)

    return left(kk), left(np.conj(kk)), left(f), left(np.conj(f))


def at(side):
    nr, nc = lax.axis_size("row"), lax.axis_size("col")
    r, c = lax.axis_index("row"), lax.axis_index("col")
    return (lax.rem(r + side[0] + nr, nr), lax.rem(c + side[1] + nc, nc))


def greet(partners):
    barrier = pltpu.get_barrier_semaphore()
    for side in partners:
        pl.semaphore_signal(barrier, inc=1, device_id=at(side), device_id_type=MESH)
    pl.semaphore_wait(barrier, len(partners))


def exists(side):
    nr, nc = lax.axis_size("row"), lax.axis_size("col")
    r, c = lax.axis_index("row") + side[0], lax.axis_index("col") + side[1]
    inside = (r >= 0) & (r < nr) & (c >= 0) & (c < nc)
    return jnp.where(inside, 1.0, 0.0).astype(F32)


def send(src, dst, sems, n, side):
    copy = pltpu.make_async_remote_copy(
        src_ref=src, dst_ref=dst, send_sem=sems.at[0, n], recv_sem=sems.at[1, n],
        device_id=at(side), device_id_type=MESH,
    )
    copy.start()
    return copy


def lanes(rows):
    return lax.broadcasted_iota(jnp.int32, (rows, N), 1)


def pack(first, second, high):
    lane = lanes(first.shape[0])
    keep = (lane >= B) if high else (lane < B)
    return jnp.where(keep, first, pltpu.roll(second, B, 1)).astype(BF16)


def rows_of(dr):
    return {-1: (0, B), 0: (0, T), 1: (T - B, B)}[dr]


def side_buffers():
    return [pltpu.VMEM((2, 4, 2, B, N), BF16), pltpu.VMEM((2, 2, T, N), BF16), pltpu.VMEM((4, 2, B, N), BF16)]


def buffer_of(buffers, n):
    return buffers[0].at[n] if n < 2 else buffers[1].at[n - 2] if n < 4 else buffers[2].at[n - 4]


def gather_kernel(obj, amps, owners, offr, offc, ext, got_amps, got_meta, s0, s1, s2, r0, r1, r2, s_amp, s_meta, sems):
    nc = lax.axis_size("col")
    me = lax.axis_index("col")
    count = amps.shape[0]
    out, into = (s0, s1, s2), (r0, r1, r2)
    for n, (dr, dc) in enumerate(SIDES):
        start, size = rows_of(dr)
        if dc == 0:
            for q in range(4):
                for j in range(2):
                    s0[n, q, j] = obj[q, start:start + size, j * N:(j + 1) * N].astype(BF16)
        else:
            j = 0 if dc < 0 else 1
            for t in range(2):
                a = obj[2 * t, start:start + size, j * N:(j + 1) * N]
                b = obj[2 * t + 1, start:start + size, j * N:(j + 1) * N]
                if n < 4:
                    s1[n - 2, t] = pack(a, b, dc > 0)
                else:
                    s2[n - 4, t] = pack(a, b, dc > 0)
    dest = [owners[0, 0, j] for j in range(count)]
    apart = [lax.rem(d - me + nc, nc) for d in dest]
    rank = []
    for j in range(count):
        same = jnp.int32(0)
        for i in range(j):
            same = same + jnp.where(dest[i] == dest[j], 1, 0)
        rank.append(same)
    lane = lax.broadcasted_iota(jnp.int32, (8, N), 1)
    for k, offset in enumerate(REACH):
        meta = jnp.zeros((8, N), jnp.int32)
        for r in range(CAP):
            which, live, row, col = jnp.int32(0), jnp.int32(0), jnp.int32(0), jnp.int32(0)
            for j in range(count):
                hit = (apart[j] == offset % nc) & (rank[j] == r)
                which = jnp.where(hit, j, which)
                live = jnp.where(hit, 1, live)
                row = jnp.where(hit, offr[0, 0, j], row)
                col = jnp.where(hit, offc[0, 0, j], col)
            s_amp[k, r] = amps[which]
            for n, value in enumerate((live, row, col)):
                meta = jnp.where(lane == 4 * r + n, value, meta)
        s_meta[k] = meta
    greet(PARTNERS)
    copies = [send(buffer_of(out, n), buffer_of(into, n), sems, n, side) for n, side in enumerate(SIDES)]
    for k, offset in enumerate(REACH):
        copies.append(send(s_meta.at[k], got_meta.at[k], sems, 8 + k, (0, offset)))
    for k, offset in enumerate(REACH):
        copies.append(send(s_amp.at[k], got_amps.at[k], sems, 15 + k, (0, offset)))
    for q in range(4):
        for j in range(2):
            ext[q, 1 + j, B:B + T] = obj[q, :, j * N:(j + 1) * N]
    for n, (dr, dc) in enumerate(SIDES):
        copies[n].wait()
        there = exists((-dr, -dc))
        start, size = {-1: (B + T, B), 0: (B, T), 1: (0, B)}[dr]
        if dc == 0:
            for q in range(4):
                for j in range(2):
                    ext[q, 1 + j, start:start + size] = r0[n, q, j].astype(F32) * there
        else:
            j = 3 if dc < 0 else 0
            for t in range(2):
                x = (r1[n - 2, t] if n < 4 else r2[n - 4, t]).astype(F32) * there
                ext[2 * t, j, start:start + size] = x
                ext[2 * t + 1, j, start:start + size] = pltpu.roll(x, B, 1)
    for copy in copies[8:]:
        copy.wait()


def gather(obj, amps, owners, offr, offc):
    vmem, smem = pl.BlockSpec(memory_space=pltpu.VMEM), pl.BlockSpec(memory_space=pltpu.SMEM)
    return pl.pallas_call(
        gather_kernel,
        out_shape=(
            jax.ShapeDtypeStruct((4, CH, EXT, N), F32),
            jax.ShapeDtypeStruct((KINDS, CAP, N, N), BF16),
            jax.ShapeDtypeStruct((KINDS, 8, N), jnp.int32),
        ),
        in_specs=[vmem, vmem, smem, smem, smem],
        out_specs=(vmem, vmem, vmem),
        scratch_shapes=[
            *side_buffers(), *side_buffers(),
            pltpu.VMEM((KINDS, CAP, N, N), BF16),
            pltpu.VMEM((KINDS, 8, N), jnp.int32),
            pltpu.SemaphoreType.DMA((2, 22)),
        ],
        compiler_params=pltpu.CompilerParams(collective_id=0, has_side_effects=True, vmem_limit_bytes=32 << 20),
    )(obj, amps, owners, offr, offc)


def dot(a, b):
    return jnp.dot(a, b, preferred_element_type=F32)


def blocks(x):
    return x[:N, :N], x[:N, N:], x[N:, :N], x[N:, N:]


def quad(a, b, c, d):
    return jnp.concatenate([jnp.concatenate([a, b], axis=1), jnp.concatenate([c, d], axis=1)], axis=0)


def turned(x):
    a, b, c, d = blocks(x.astype(BF16))
    return quad(a, c, b, d)


def window(ext, q, row, base, shift):
    low = ext[q, base, pl.ds(row, N), :]
    high = ext[q, base + 1, pl.ds(row, N), :]
    return pltpu.roll(jnp.where(lanes(N) >= shift, low, high), N - shift, 1)


def forward(w, probe, kl, kr, fl, fr):
    psi = [(w[0] * probe[m, 0] - w[1] * probe[m, 1], w[0] * probe[m, 1] + w[1] * probe[m, 0]) for m in range(2)]
    x = quad(psi[0][0], psi[1][0], psi[0][1], psi[1][1]).astype(BF16)
    phi = dot(turned(dot(kl, x)), kr)
    a, b, c, d = blocks(phi)
    x = quad(a * w[2] - b * w[3], c * w[2] - d * w[3], a * w[3] + b * w[2], c * w[3] + d * w[2]).astype(BF16)
    return phi, dot(turned(dot(fl, x)), fr)


def backward(phi, far, amp, live, w2, probe, kl, kr, fl, fr):
    a, b, c, d = blocks(far)
    inten = (a * a + b * b) + (c * c + d * d)
    factor = live * (1.0 - amp * lax.rsqrt(jnp.maximum(inten, 1.0)))
    x = quad(a * factor, c * factor, b * factor, d * factor).astype(BF16)
    g2 = dot(turned(dot(fr, x)), fl)
    a, b, c, d = blocks(g2)
    wr, wi = w2
    x = quad(wr * a + wi * b, wr * c + wi * d, wr * b - wi * a, wr * d - wi * c).astype(BF16)
    pa, pb, pc, pd = blocks(phi)
    s2r = pa * a + pb * b + pc * c + pd * d
    s2i = pa * b - pb * a + pc * d - pd * c
    g1 = dot(turned(dot(kr, x)), kl)
    a, b, c, d = blocks(g1)
    s1r = probe[0, 0] * a + probe[0, 1] * b + probe[1, 0] * c + probe[1, 1] * d
    s1i = probe[0, 0] * b - probe[0, 1] * a + probe[1, 0] * d - probe[1, 1] * c
    return s1r, s1i, s2r, s2i


def positions_kernel(meta, ext, amps, probe, kl, kr, fl, fr, acc, order):
    acc[...] = jnp.zeros_like(acc)
    mats = (kl, kr, fl, fr)
    order[SLOTS] = 0
    count = jnp.int32(0)
    for i in range(SLOTS):
        order[count] = i
        count = count + meta[i // CAP, 0, 4 * (i % CAP)]
    order[count] = SLOTS

    def step(pair, carry):
        items = []
        for n in range(2):
            slot = order[2 * pair + n]
            live = jnp.where(slot < SLOTS, 1, 0)
            slot = jnp.minimum(slot, SLOTS - 1)
            kind, rank = slot // CAP, lax.rem(slot, CAP)
            row = meta[kind, 0, 4 * rank + 1] * live
            col = meta[kind, 0, 4 * rank + 2] * live + B
            base, shift = col // N, lax.rem(col, N)
            items.append((kind, rank, live.astype(F32), row, base, shift))
        ks = [m[...] for m in mats]
        ws = [[window(ext, q, row, base, shift) for q in range(4)] for _, _, _, row, base, shift in items]
        fw = [forward(w, probe, *ks) for w in ws]
        gs = [
            backward(*fw[n], amps[kind, rank].astype(F32), live, ws[n][2:], probe, *ks)
            for n, (kind, rank, live, _, _, _) in enumerate(items)
        ]
        for g, (_, _, _, row, base, shift) in zip(gs, items):
            for q in range(4):
                t = pltpu.roll(g[q], shift, 1)
                low = lanes(N) >= shift
                acc[q, base, pl.ds(row, N), :] += jnp.where(low, t, 0.0)
                acc[q, base + 1, pl.ds(row, N), :] += jnp.where(low, 0.0, t)
        return carry

    lax.fori_loop(0, (count + 1) // 2, step, 0)


def positions(meta, ext, amps, probe, mats):
    vmem, smem = pl.BlockSpec(memory_space=pltpu.VMEM), pl.BlockSpec(memory_space=pltpu.SMEM)
    return pl.pallas_call(
        positions_kernel,
        out_shape=jax.ShapeDtypeStruct((4, CH, EXT, N), F32),
        in_specs=[smem] + [vmem] * 7,
        out_specs=vmem,
        scratch_shapes=[pltpu.SMEM((SLOTS + 2,), jnp.int32)],
        compiler_params=pltpu.CompilerParams(vmem_limit_bytes=32 << 20),
    )(meta, ext, amps, probe, *mats)


def fold_kernel(acc, out, s0, s1, s2, r0, r1, r2, sems):
    send_to, into = (s0, s1, s2), (r0, r1, r2)
    for n, (dr, dc) in enumerate(SIDES):
        start, size = {-1: (0, B), 0: (B, T), 1: (B + T, B)}[dr]
        if dc == 0:
            for q in range(4):
                for j in range(2):
                    s0[n, q, j] = acc[q, 1 + j, start:start + size].astype(BF16)
        else:
            j = 0 if dc < 0 else 3
            for t in range(2):
                x = pack(acc[2 * t, j, start:start + size], acc[2 * t + 1, j, start:start + size], dc < 0)
                if n < 4:
                    s1[n - 2, t] = x
                else:
                    s2[n - 4, t] = x
    greet(SIDES)
    copies = [send(buffer_of(send_to, n), buffer_of(into, n), sems, n, side) for n, side in enumerate(SIDES)]
    for q in range(4):
        for j in range(2):
            out[q, :, j * N:(j + 1) * N] = acc[q, 1 + j, B:B + T]
    for n, (dr, dc) in enumerate(SIDES):
        copies[n].wait()
        there = exists((-dr, -dc))
        start, size = {-1: (T - B, B), 0: (0, T), 1: (0, B)}[dr]
        if dc == 0:
            for q in range(4):
                for j in range(2):
                    out[q, start:start + size, j * N:(j + 1) * N] += r0[n, q, j].astype(F32) * there
        else:
            j = 1 if dc < 0 else 0
            for t in range(2):
                x = (r1[n - 2, t] if n < 4 else r2[n - 4, t]).astype(F32) * there
                lane = lanes(size)
                mine = (lane >= B) if dc < 0 else (lane < B)
                out[2 * t, start:start + size, j * N:(j + 1) * N] += jnp.where(mine, x, 0.0)
                out[2 * t + 1, start:start + size, j * N:(j + 1) * N] += jnp.where(mine, pltpu.roll(x, B, 1), 0.0)


def fold(acc):
    vmem = pl.BlockSpec(memory_space=pltpu.VMEM)
    return pl.pallas_call(
        fold_kernel,
        out_shape=jax.ShapeDtypeStruct((4, T, T), F32),
        in_specs=[vmem],
        out_specs=vmem,
        scratch_shapes=[*side_buffers(), *side_buffers(), pltpu.SemaphoreType.DMA((2, 8))],
        compiler_params=pltpu.CompilerParams(collective_id=1, has_side_effects=True, vmem_limit_bytes=32 << 20),
    )(acc)


def local(objects, probe, amplitudes, owners, off_rows, off_cols):
    mats = tables()
    ext, amps, meta = gather(objects.reshape(4, T, T), amplitudes.reshape(-1, N, N), owners, off_rows, off_cols)
    acc = positions(meta, ext, amps, probe, mats)
    return fold(acc).reshape(objects.shape)


def solution(mesh):
    placed = (
        P(None, None, "row", "col"),
        P(),
        P("row", "col", None, None, None),
        P("row", "col", None),
        P("row", "col", None),
        P("row", "col", None),
    )
    return jax.shard_map(
        local, mesh=mesh, in_specs=placed, out_specs=P(None, None, "row", "col"), check_vma=False
    )
```

```python
import math

import jax
import jax.numpy as jnp
import numpy as np
from jax import lax
from jax.experimental import pallas as pl
from jax.experimental.pallas import tpu as pltpu
from jax.sharding import PartitionSpec as P

MESH = pl.DeviceIdType.MESH
REACH = (-3, -2, -1, 1, 2, 3, 4)
KINDS = len(REACH)
CAP = 2
SLOTS = CAP * KINDS
RMAX = 12
COUNT = 6
FRESNEL = 24.0
F32 = jnp.float32
BF16 = jnp.bfloat16
N = 128
B = 64
T = 256
EXT = T + 2 * B
CH = 4
SIDES = ((-1, 0), (1, 0), (0, -1), (0, 1), (-1, -1), (-1, 1), (1, -1), (1, 1))
PARTNERS = SIDES + tuple((0, d) for d in (-4, -3, -2, 2, 3, 4))
GROUP = 3


def tables():
    k = np.arange(N)
    f = np.exp(-2j * np.pi * ((k[:, None] * k[None, :]) % N) / N) / math.sqrt(N)
    c = (k + N // 2) % N - N // 2
    d = np.exp(-1j * np.pi * FRESNEL * c * c / (N * N))
    kk = np.conj(f) @ (d[:, None] * f)

    def left(a):
        return np.block([[a.real, -a.imag], [a.imag, a.real]]).astype(np.float32)

    return jnp.asarray(np.stack([left(kk), left(np.conj(kk)), left(f), left(np.conj(f))])).astype(BF16)


def at(side):
    nr, nc = lax.axis_size("row"), lax.axis_size("col")
    r, c = lax.axis_index("row"), lax.axis_index("col")
    return (lax.rem(r + side[0] + nr, nr), lax.rem(c + side[1] + nc, nc))


def exists(side):
    nr, nc = lax.axis_size("row"), lax.axis_size("col")
    r, c = lax.axis_index("row") + side[0], lax.axis_index("col") + side[1]
    inside = (r >= 0) & (r < nr) & (c >= 0) & (c < nc)
    return jnp.where(inside, 1.0, 0.0).astype(F32)


def lanes(rows):
    return lax.broadcasted_iota(jnp.int32, (rows, N), 1)


def pack(first, second, high):
    lane = lanes(first.shape[0])
    keep = (lane >= B) if high else (lane < B)
    return jnp.where(keep, first, pltpu.roll(second, B, 1)).astype(BF16)


def side_buffers():
    return [pltpu.VMEM((2, 2, 2, 2, B, N), BF16), pltpu.VMEM((2, 2, T, N), BF16), pltpu.VMEM((4, 2, B, N), BF16)]


def buffer_of(buffers, n, s):
    return buffers[0].at[n, s] if n < 2 else buffers[1].at[n - 2, s] if n < 4 else buffers[2].at[n - 4, s]


def dot(a, b):
    return jnp.dot(a, b, preferred_element_type=F32)


def blocks(x):
    return x[:N, :N], x[:N, N:], x[N:, :N], x[N:, N:]


def quad(a, b, c, d):
    return jnp.concatenate([jnp.concatenate([a, b], axis=1), jnp.concatenate([c, d], axis=1)], axis=0)


def both(left, x, right):
    a, b, c, d = blocks(dot(left, x).astype(BF16))
    return dot(quad(a, c, b, d), right)


def kernel(
    obj_h, amps_h, own_h, offr_h, offc_h, probe_h, mats_h, out_h,
    obj, amps, own, offr, offc, probe, mats, out,
    ext, s0, s1, s2, r0, r1, r2, f0, f1, f2, g0, g1, g2,
    s_amp, got_amp, s_meta, got_meta, meta, plan, masks, phi, far, win, gphi, tbuf, acc,
    sems, lsems,
):
    nc = lax.axis_size("col")
    me = lax.axis_index("col")
    used = [0]

    def send(src, dst, side):
        n = used[0]
        used[0] += 1
        copy = pltpu.make_async_remote_copy(
            src_ref=src, dst_ref=dst, send_sem=sems.at[0, n], recv_sem=sems.at[1, n],
            device_id=at(side), device_id_type=MESH,
        )
        copy.start()
        return copy

    barrier = pltpu.get_barrier_semaphore()
    for side in PARTNERS:
        pl.semaphore_signal(barrier, inc=1, device_id=at(side), device_id_type=MESH)

    def fetch(n, src, dst):
        copy = pltpu.make_async_copy(src, dst, lsems.at[n])
        copy.start()
        return copy

    in_ints = [fetch(n, a, b) for n, (a, b) in enumerate(((own_h, own), (offr_h, offr), (offc_h, offc)))]
    in_obj = [fetch(3 + s, obj_h.at[pl.ds(2 * s, 2)], obj.at[pl.ds(2 * s, 2)]) for s in range(2)]
    in_amps = fetch(5, amps_h, amps)
    in_probe, in_mats = fetch(6, probe_h, probe), fetch(7, mats_h, mats)

    for copy in in_ints:
        copy.wait()
    dest = [own[0, 0, j] for j in range(COUNT)]
    apart = [lax.rem(d - me + nc, nc) for d in dest]
    rank = []
    for j in range(COUNT):
        same = jnp.int32(0)
        for i in range(j):
            same = same + jnp.where(dest[i] == dest[j], 1, 0)
        rank.append(same)
    chosen = []
    lane8 = lanes(8)
    for k, offset in enumerate(REACH):
        line = jnp.zeros((8, N), jnp.int32)
        for r in range(CAP):
            which, live, row, col = jnp.int32(0), jnp.int32(0), jnp.int32(0), jnp.int32(0)
            for j in range(COUNT):
                hit = (apart[j] == offset % nc) & (rank[j] == r)
                which = jnp.where(hit, j, which)
                live = jnp.where(hit, 1, live)
                row = jnp.where(hit, offr[0, 0, j], row)
                col = jnp.where(hit, offc[0, 0, j], col)
            chosen.append(which)
            for n, value in enumerate((live, row, col)):
                line = jnp.where(lane8 == 4 * r + n, value, line)
        s_meta[k] = line

    def pack_object(s):
        for n, (dr, dc) in enumerate(SIDES):
            start, size = {-1: (0, B), 0: (0, T), 1: (T - B, B)}[dr]
            if dc == 0:
                for q in range(2):
                    for j in range(2):
                        s0[n, s, q, j] = obj[2 * s + q, start:start + size, j * N:(j + 1) * N].astype(BF16)
            else:
                j = 0 if dc < 0 else 1
                a = obj[2 * s, start:start + size, j * N:(j + 1) * N]
                b = obj[2 * s + 1, start:start + size, j * N:(j + 1) * N]
                if n < 4:
                    s1[n - 2, s] = pack(a, b, dc > 0)
                else:
                    s2[n - 4, s] = pack(a, b, dc > 0)

    in_obj[0].wait()
    pack_object(0)
    pl.semaphore_wait(barrier, len(PARTNERS))
    meta_copies = [send(s_meta.at[k], got_meta.at[k], (0, offset)) for k, offset in enumerate(REACH)]
    halo = [[send(buffer_of((s0, s1, s2), n, 0), buffer_of((r0, r1, r2), n, 0), side) for n, side in enumerate(SIDES)]]
    in_obj[1].wait()
    pack_object(1)
    halo.append([send(buffer_of((s0, s1, s2), n, 1), buffer_of((r0, r1, r2), n, 1), side) for n, side in enumerate(SIDES)])

    in_amps.wait()
    for k in range(KINDS):
        for r in range(CAP):
            s_amp[k, r] = amps[chosen[CAP * k + r]]
    for q in range(4):
        for j in range(2):
            ext[q, 1 + j, B:B + T] = obj[q, :, j * N:(j + 1) * N]

    def clear(n, carry):
        for q in range(4):
            tbuf[n, q, 0:T] = jnp.zeros((T, N), F32)
            tbuf[n, q, T + N:] = jnp.zeros((T, N), F32)
        return carry

    lax.fori_loop(0, RMAX, clear, 0)
    in_probe.wait()
    in_mats.wait()
    for copy in meta_copies:
        copy.wait()
    to_smem = fetch(8, got_meta, meta)
    to_smem.wait()

    lives = [meta[i // CAP, 0, 4 * (i % CAP)] for i in range(SLOTS)]
    places, total = [], jnp.int32(0)
    for live in lives:
        places.append(total)
        total = total + live
    for p in range(RMAX):
        slot, live = jnp.int32(0), jnp.int32(0)
        for i in range(SLOTS):
            hit = (places[i] == p) & (lives[i] == 1)
            slot = jnp.where(hit, i, slot)
            live = jnp.where(hit, 1, live)
        kind, rank_in = slot // CAP, lax.rem(slot, CAP)
        row = meta[kind, 0, 4 * rank_in + 1] * live
        col = meta[kind, 0, 4 * rank_in + 2] * live + B
        base, shift = col // N, lax.rem(col, N)
        for n, value in enumerate((kind, rank_in, live, row, base, shift)):
            plan[p, n] = value
        for k in range(CH):
            low = jnp.where(base == k, 1.0, 0.0).astype(F32)
            high = jnp.where(base + 1 == k, 1.0, 0.0).astype(F32)
            masks[p, k] = jnp.where(lane8 >= shift, low, high)

    def unpack_object(s):
        for n, (dr, dc) in enumerate(SIDES):
            halo[s][n].wait()
            there = exists((-dr, -dc))
            start, size = {-1: (B + T, B), 0: (B, T), 1: (0, B)}[dr]
            if dc == 0:
                for q in range(2):
                    for j in range(2):
                        ext[2 * s + q, 1 + j, start:start + size] = r0[n, s, q, j].astype(F32) * there
            else:
                j = 3 if dc < 0 else 0
                x = (r1[n - 2, s] if n < 4 else r2[n - 4, s]).astype(F32) * there
                ext[2 * s, j, start:start + size] = x
                ext[2 * s + 1, j, start:start + size] = pltpu.roll(x, B, 1)

    def window(q, p):
        row, base, shift = plan[p, 3], plan[p, 4], plan[p, 5]
        low = ext[q, base, pl.ds(row, N), :]
        high = ext[q, base + 1, pl.ds(row, N), :]
        return pltpu.roll(jnp.where(lanes(N) >= shift, low, high), N - shift, 1)

    def each(work):
        def step(n, carry):
            for i in range(GROUP):
                work(n * GROUP + i)
            return carry

        lax.fori_loop(0, RMAX // GROUP, step, 0)

    def first(p):
        wr, wi = window(0, p), window(1, p)
        psi = [(wr * probe[m, 0] - wi * probe[m, 1], wr * probe[m, 1] + wi * probe[m, 0]) for m in range(2)]
        x = quad(psi[0][0], psi[1][0], psi[0][1], psi[1][1]).astype(BF16)
        phi[p] = both(mats[0], x, mats[1])

    def second(p):
        wr, wi = window(2, p), window(3, p)
        win[p, 0], win[p, 1] = wr, wi
        a, b, c, d = blocks(phi[p])
        x = quad(a * wr - b * wi, c * wr - d * wi, a * wi + b * wr, c * wi + d * wr).astype(BF16)
        far[p] = both(mats[2], x, mats[3])

    def third(p):
        amp = got_amp[plan[p, 0], plan[p, 1]].astype(F32)
        live = plan[p, 2].astype(F32)
        a, b, c, d = blocks(far[p])
        inten = (a * a + b * b) + (c * c + d * d)
        factor = live * (1.0 - amp * lax.rsqrt(jnp.maximum(inten, 1.0)))
        x = quad(a * factor, c * factor, b * factor, d * factor).astype(BF16)
        a, b, c, d = blocks(both(mats[3], x, mats[2]))
        wr, wi = win[p, 0], win[p, 1]
        gphi[p] = quad(wr * a + wi * b, wr * c + wi * d, wr * b - wi * a, wr * d - wi * c).astype(BF16)
        pa, pb, pc, pd = blocks(phi[p])
        shift = plan[p, 5]
        tbuf[p, 2, T:T + N] = pltpu.roll(pa * a + pb * b + pc * c + pd * d, shift, 1)
        tbuf[p, 3, T:T + N] = pltpu.roll(pa * b - pb * a + pc * d - pd * c, shift, 1)

    def fourth(p):
        a, b, c, d = blocks(both(mats[1], gphi[p], mats[0]))
        shift = plan[p, 5]
        tbuf[p, 0, T:T + N] = pltpu.roll(probe[0, 0] * a + probe[0, 1] * b + probe[1, 0] * c + probe[1, 1] * d, shift, 1)
        tbuf[p, 1, T:T + N] = pltpu.roll(probe[0, 0] * b - probe[0, 1] * a + probe[1, 0] * d - probe[1, 1] * c, shift, 1)

    def scatter(s):
        def step(n, carry):
            q, start = 2 * s + n // (EXT // B), lax.rem(n, EXT // B) * B
            sums = [jnp.zeros((B // 8, 8, N), F32) for _ in range(CH)]
            for p in range(RMAX):
                t = tbuf[p, q, pl.ds(T - plan[p, 3] + start, B), :].reshape(B // 8, 8, N)
                for k in range(CH):
                    sums[k] = sums[k] + t * masks[p, k]
            for k in range(CH):
                acc[q, k, pl.ds(pl.multiple_of(start, B), B), :] = sums[k].reshape(B, N)
            return carry

        lax.fori_loop(0, 2 * (EXT // B), step, 0)

    def send_border(s):
        for n, (dr, dc) in enumerate(SIDES):
            start, size = {-1: (0, B), 0: (B, T), 1: (B + T, B)}[dr]
            if dc == 0:
                for q in range(2):
                    for j in range(2):
                        f0[n, s, q, j] = acc[2 * s + q, 1 + j, start:start + size].astype(BF16)
            else:
                j = 0 if dc < 0 else 3
                x = pack(acc[2 * s, j, start:start + size], acc[2 * s + 1, j, start:start + size], dc < 0)
                if n < 4:
                    f1[n - 2, s] = x
                else:
                    f2[n - 4, s] = x
        return [send(buffer_of((f0, f1, f2), n, s), buffer_of((g0, g1, g2), n, s), side) for n, side in enumerate(SIDES)]

    def add_border(s, copies):
        for q in range(2):
            for j in range(2):
                out[2 * s + q, :, j * N:(j + 1) * N] = acc[2 * s + q, 1 + j, B:B + T]
        for n, (dr, dc) in enumerate(SIDES):
            copies[n].wait()
            there = exists((-dr, -dc))
            start, size = {-1: (T - B, B), 0: (0, T), 1: (0, B)}[dr]
            if dc == 0:
                for q in range(2):
                    for j in range(2):
                        out[2 * s + q, start:start + size, j * N:(j + 1) * N] += g0[n, s, q, j].astype(F32) * there
            else:
                j = 1 if dc < 0 else 0
                x = (g1[n - 2, s] if n < 4 else g2[n - 4, s]).astype(F32) * there
                lane = lanes(size)
                mine = (lane >= B) if dc < 0 else (lane < B)
                out[2 * s, start:start + size, j * N:(j + 1) * N] += jnp.where(mine, x, 0.0)
                out[2 * s + 1, start:start + size, j * N:(j + 1) * N] += jnp.where(mine, pltpu.roll(x, B, 1), 0.0)

    unpack_object(0)
    amp_copies = [send(s_amp.at[k], got_amp.at[k], (0, offset)) for k, offset in enumerate(REACH)]
    each(first)
    unpack_object(1)
    each(second)
    for copy in amp_copies:
        copy.wait()
    each(third)
    scatter(1)
    late = send_border(1)
    each(fourth)
    scatter(0)
    last = send_border(0)
    add_border(1, late)
    back = [fetch(9, out.at[pl.ds(2, 2)], out_h.at[pl.ds(2, 2)])]
    add_border(0, last)
    back.append(fetch(10, out.at[pl.ds(0, 2)], out_h.at[pl.ds(0, 2)]))
    for copy in back:
        copy.wait()


def local(objects, probe, amplitudes, owners, off_rows, off_cols):
    anywhere = pl.BlockSpec(memory_space=pl.ANY)
    vmem, smem = pltpu.VMEM, pltpu.SMEM
    i32 = jnp.int32
    gradient = pl.pallas_call(
        kernel,
        out_shape=jax.ShapeDtypeStruct((4, T, T), F32),
        in_specs=[anywhere] * 7,
        out_specs=anywhere,
        scratch_shapes=[
            vmem((4, T, T), F32), vmem((COUNT, N, N), BF16), *[smem((1, 1, COUNT), i32)] * 3,
            vmem((2, 2, N, N), F32), vmem((4, 2 * N, 2 * N), BF16), vmem((4, T, T), F32),
            vmem((4, CH, EXT, N), F32), *side_buffers(), *side_buffers(), *side_buffers(), *side_buffers(),
            vmem((KINDS, CAP, N, N), BF16), vmem((KINDS, CAP, N, N), BF16),
            vmem((KINDS, 8, N), i32), vmem((KINDS, 8, N), i32), smem((KINDS, 8, N), i32), smem((RMAX, 8), i32),
            vmem((RMAX, CH, 8, N), F32), vmem((RMAX, 2 * N, 2 * N), F32), vmem((RMAX, 2 * N, 2 * N), F32),
            vmem((RMAX, 2, N, N), F32), vmem((RMAX, 2 * N, 2 * N), BF16),
            vmem((RMAX, 4, 2 * T + N, N), F32), vmem((4, CH, EXT, N), F32),
            pltpu.SemaphoreType.DMA((2, 2 * KINDS + 4 * len(SIDES))), pltpu.SemaphoreType.DMA((11,)),
        ],
        compiler_params=pltpu.CompilerParams(collective_id=0, has_side_effects=True, vmem_limit_bytes=56 << 20),
    )(objects.reshape(4, T, T), amplitudes.reshape(COUNT, N, N), owners, off_rows, off_cols, probe, tables())
    return gradient.reshape(objects.shape)


def solution(mesh):
    placed = (
        P(None, None, "row", "col"),
        P(),
        P("row", "col", None, None, None),
        P("row", "col", None),
        P("row", "col", None),
        P("row", "col", None),
    )
    return jax.shard_map(
        local, mesh=mesh, in_specs=placed, out_specs=P(None, None, "row", "col"), check_vma=False
    )
```

```python
import math

import jax
import jax.numpy as jnp
import numpy as np
from jax import lax
from jax.experimental import pallas as pl
from jax.experimental.pallas import tpu as pltpu
from jax.sharding import PartitionSpec as P

MESH = pl.DeviceIdType.MESH
REACH = (-3, -2, -1, 1, 2, 3, 4)
KINDS = len(REACH)
CAP = 2
SLOTS = CAP * KINDS
RMAX = 12
COUNT = 6
FRESNEL = 24.0
F32 = jnp.float32
BF16 = jnp.bfloat16
N = 128
B = 64
T = 256
EXT = T + 2 * B
CH = 4
SIDES = ((-1, 0), (1, 0), (0, -1), (0, 1), (-1, -1), (-1, 1), (1, -1), (1, 1))
XS = 8
PARTNERS = SIDES + tuple((0, d) for d in (-4, -3, -2, 2, 3, 4, -XS, XS))
THIRDS = 3
GROUP = 6


def tables():
    k = np.arange(N)
    f = np.exp(-2j * np.pi * ((k[:, None] * k[None, :]) % N) / N) / math.sqrt(N)
    c = (k + N // 2) % N - N // 2
    d = np.exp(-1j * np.pi * FRESNEL * c * c / (N * N))
    kk = np.conj(f) @ (d[:, None] * f)

    def left(a):
        return np.block([[a.real, -a.imag], [a.imag, a.real]]).astype(np.float32)

    return jnp.asarray(np.stack([left(kk), left(np.conj(kk)), left(f), left(np.conj(f))])).astype(BF16)


def at(side):
    nr, nc = lax.axis_size("row"), lax.axis_size("col")
    r, c = lax.axis_index("row"), lax.axis_index("col")
    return (lax.rem(r + side[0] + nr, nr), lax.rem(c + side[1] + nc, nc))


def exists(side):
    nr, nc = lax.axis_size("row"), lax.axis_size("col")
    r, c = lax.axis_index("row") + side[0], lax.axis_index("col") + side[1]
    inside = (r >= 0) & (r < nr) & (c >= 0) & (c < nc)
    return jnp.where(inside, 1.0, 0.0).astype(F32)


def lanes(rows):
    return lax.broadcasted_iota(jnp.int32, (rows, N), 1)


def pack(first, second, high):
    lane = lanes(first.shape[0])
    keep = (lane >= B) if high else (lane < B)
    return jnp.where(keep, first, pltpu.roll(second, B, 1)).astype(BF16)


def side_buffers():
    return [pltpu.VMEM((2, 2, 2, 2, B, N), BF16), pltpu.VMEM((2, 2, T, N), BF16), pltpu.VMEM((4, 2, B, N), BF16)]


def buffer_of(buffers, n, s):
    return buffers[0].at[n, s] if n < 2 else buffers[1].at[n - 2, s] if n < 4 else buffers[2].at[n - 4, s]


def dot(a, b):
    return jnp.dot(a, b, preferred_element_type=F32)


def blocks(x):
    return x[:N, :N], x[:N, N:], x[N:, :N], x[N:, N:]


def quad(a, b, c, d):
    return jnp.concatenate([jnp.concatenate([a, b], axis=1), jnp.concatenate([c, d], axis=1)], axis=0)


def both(left, x, right):
    a, b, c, d = blocks(dot(left, x).astype(BF16))
    return dot(quad(a, c, b, d), right)


def kernel(
    obj_h, amps_h, own_h, offr_h, offc_h, probe_h, mats_h, out_h,
    obj, amps, own, offr, offc, probe, mats, out,
    ext, s0, s1, s2, r0, r1, r2, f0, f1, f2, g0, g1, g2,
    s_amp, got_amp, passing, s_meta, got_meta, meta, plan, masks, phi, far, win, gphi, rows, parts, acc,
    sems, lsems,
):
    nc = lax.axis_size("col")
    me = lax.axis_index("col")
    used = [0]

    def prepare(src, dst, side, arrival=None):
        n = used[0]
        used[0] += 1
        return pltpu.make_async_remote_copy(
            src_ref=src, dst_ref=dst, send_sem=sems.at[0, n], recv_sem=sems.at[1, n if arrival is None else arrival],
            device_id=at(side), device_id_type=MESH,
        )

    def send(src, dst, side):
        copy = prepare(src, dst, side)
        copy.start()
        return copy

    barrier = pltpu.get_barrier_semaphore()
    for side in PARTNERS:
        pl.semaphore_signal(barrier, inc=1, device_id=at(side), device_id_type=MESH)

    def fetch(n, src, dst):
        copy = pltpu.make_async_copy(src, dst, lsems.at[n])
        copy.start()
        return copy

    in_ints = [fetch(n, a, b) for n, (a, b) in enumerate(((own_h, own), (offr_h, offr), (offc_h, offc)))]
    in_obj = [fetch(3 + s, obj_h.at[pl.ds(2 * s, 2)], obj.at[pl.ds(2 * s, 2)]) for s in range(2)]
    in_amps = fetch(5, amps_h, amps)
    in_probe, in_mats = fetch(6, probe_h, probe), fetch(7, mats_h, mats)

    def pack_object(s):
        for n, (dr, dc) in enumerate(SIDES):
            start, size = {-1: (0, B), 0: (0, T), 1: (T - B, B)}[dr]
            if dc == 0:
                for q in range(2):
                    for j in range(2):
                        s0[n, s, q, j] = obj[2 * s + q, start:start + size, j * N:(j + 1) * N].astype(BF16)
            else:
                j = 0 if dc < 0 else 1
                a = obj[2 * s, start:start + size, j * N:(j + 1) * N]
                b = obj[2 * s + 1, start:start + size, j * N:(j + 1) * N]
                if n < 4:
                    s1[n - 2, s] = pack(a, b, dc > 0)
                else:
                    s2[n - 4, s] = pack(a, b, dc > 0)

    in_obj[0].wait()
    pack_object(0)
    pl.semaphore_wait(barrier, len(PARTNERS))
    halo = [[send(buffer_of((s0, s1, s2), n, 0), buffer_of((r0, r1, r2), n, 0), side) for n, side in enumerate(SIDES)]]
    in_obj[1].wait()
    pack_object(1)
    halo.append([send(buffer_of((s0, s1, s2), n, 1), buffer_of((r0, r1, r2), n, 1), side) for n, side in enumerate(SIDES)])

    for copy in in_ints:
        copy.wait()
    dest = [own[0, 0, j] for j in range(COUNT)]
    apart = [lax.rem(d - me + nc, nc) for d in dest]
    rank = []
    for j in range(COUNT):
        same = jnp.int32(0)
        for i in range(j):
            same = same + jnp.where(dest[i] == dest[j], 1, 0)
        rank.append(same)
    chosen = []
    lane8 = lanes(8)
    for k, offset in enumerate(REACH):
        line = jnp.zeros((8, N), jnp.int32)
        for r in range(CAP):
            which, live, row, col = jnp.int32(0), jnp.int32(0), jnp.int32(0), jnp.int32(0)
            for j in range(COUNT):
                hit = (apart[j] == offset % nc) & (rank[j] == r)
                which = jnp.where(hit, j, which)
                live = jnp.where(hit, 1, live)
                row = jnp.where(hit, offr[0, 0, j], row)
                col = jnp.where(hit, offc[0, 0, j], col)
            chosen.append(which)
            for n, value in enumerate((live, row, col)):
                line = jnp.where(lane8 == 4 * r + n, value, line)
        s_meta[k] = line

    meta_copies = [send(s_meta.at[k], got_meta.at[k], (0, offset)) for k, offset in enumerate(REACH)]
    in_amps.wait()
    for k in range(KINDS):
        for r in range(CAP):
            s_amp[k, r] = amps[chosen[CAP * k + r]]

    x = lax.rem(me, XS)
    straight, detour, onward, turns = [], [], [], []
    for k, offset in enumerate(REACH):
        step = XS if offset > 0 else -XS
        turns.append(x == (XS - offset if offset > 0 else -1 - offset))
        arrival = used[0]
        straight.append(prepare(s_amp.at[k], got_amp.at[k], (0, offset)))
        detour.append(prepare(s_amp.at[k], passing, (0, step)))
        onward.append(prepare(passing, got_amp.at[k], (0, offset - step), arrival))

    def start_amps():
        for k in range(KINDS):
            @pl.when(turns[k])
            def _():
                detour[k].start()

            @pl.when(jnp.logical_not(turns[k]))
            def _():
                straight[k].start()

    def pass_on():
        for k in range(KINDS):
            @pl.when(turns[k])
            def _():
                detour[k].wait_recv()
                onward[k].start()

    def end_amps():
        for k in range(KINDS):
            straight[k].wait_recv()

            @pl.when(turns[k])
            def _():
                detour[k].wait_send()
                onward[k].wait_send()

            @pl.when(jnp.logical_not(turns[k]))
            def _():
                straight[k].wait_send()

    start_amps()

    for q in range(4):
        for j in range(2):
            ext[q, 1 + j, B:B + T] = obj[q, :, j * N:(j + 1) * N]

    in_probe.wait()
    in_mats.wait()
    for copy in meta_copies:
        copy.wait()
    to_smem = fetch(8, got_meta, meta)
    to_smem.wait()

    lives = [meta[i // CAP, 0, 4 * (i % CAP)] for i in range(SLOTS)]
    places, total = [], jnp.int32(0)
    for live in lives:
        places.append(total)
        total = total + live
    for p in range(RMAX):
        slot, live = jnp.int32(0), jnp.int32(0)
        for i in range(SLOTS):
            hit = (places[i] == p) & (lives[i] == 1)
            slot = jnp.where(hit, i, slot)
            live = jnp.where(hit, 1, live)
        kind, rank_in = slot // CAP, lax.rem(slot, CAP)
        row = meta[kind, 0, 4 * rank_in + 1] * live
        col = meta[kind, 0, 4 * rank_in + 2] * live + B
        base, shift = col // N, lax.rem(col, N)
        for n, value in enumerate((kind, rank_in, live, row, base, shift)):
            plan[p, n] = value
        for k in range(THIRDS):
            low = jnp.where(base == k, 1.0, 0.0).astype(F32)
            high = jnp.where((base + 1 == k) | (base + 1 == k + THIRDS), 1.0, 0.0).astype(F32)
            masks[p, k] = jnp.where(lane8 >= shift, low, high)
        away = lax.broadcasted_iota(jnp.int32, (EXT, N), 0) - lanes(EXT)
        rows[:, p * N:(p + 1) * N] = jnp.where(away == row, 1.0, 0.0).astype(BF16)

    def unpack_object(s):
        for n, (dr, dc) in enumerate(SIDES):
            halo[s][n].wait()
            there = exists((-dr, -dc))
            start, size = {-1: (B + T, B), 0: (B, T), 1: (0, B)}[dr]
            if dc == 0:
                for q in range(2):
                    for j in range(2):
                        ext[2 * s + q, 1 + j, start:start + size] = r0[n, s, q, j].astype(F32) * there
            else:
                j = 3 if dc < 0 else 0
                x = (r1[n - 2, s] if n < 4 else r2[n - 4, s]).astype(F32) * there
                ext[2 * s, j, start:start + size] = x
                ext[2 * s + 1, j, start:start + size] = pltpu.roll(x, B, 1)

    def window(q, p):
        row, base, shift = plan[p, 3], plan[p, 4], plan[p, 5]
        low = ext[q, base, pl.ds(row, N), :]
        high = ext[q, base + 1, pl.ds(row, N), :]
        return pltpu.roll(jnp.where(lanes(N) >= shift, low, high), N - shift, 1)

    def each(work):
        def step(n, carry):
            for i in range(GROUP):
                work(n * GROUP + i)
            return carry

        lax.fori_loop(0, RMAX // GROUP, step, 0)

    def first(p):
        wr, wi = window(0, p), window(1, p)
        psi = [(wr * probe[m, 0] - wi * probe[m, 1], wr * probe[m, 1] + wi * probe[m, 0]) for m in range(2)]
        x = quad(psi[0][0], psi[1][0], psi[0][1], psi[1][1]).astype(BF16)
        phi[p] = both(mats[0], x, mats[1])

    def second(p):
        wr, wi = window(2, p), window(3, p)
        win[p, 0], win[p, 1] = wr, wi
        a, b, c, d = blocks(phi[p])
        x = quad(a * wr - b * wi, c * wr - d * wi, a * wi + b * wr, c * wi + d * wr).astype(BF16)
        far[p] = both(mats[2], x, mats[3])

    def place(p, q, grad):
        t = pltpu.roll(grad, plan[p, 5], 1).reshape(N // 8, 8, N)
        for k in range(THIRDS):
            at_k = (t * masks[p, k]).reshape(N, N).astype(BF16)
            start = pl.multiple_of(p * N, N)
            parts[pl.ds(start, N), (THIRDS * q + k) * N:(THIRDS * q + k + 1) * N] = at_k

    def third(p):
        amp = got_amp[plan[p, 0], plan[p, 1]].astype(F32)
        live = plan[p, 2].astype(F32)
        a, b, c, d = blocks(far[p])
        inten = (a * a + b * b) + (c * c + d * d)
        factor = live * (1.0 - amp * lax.rsqrt(jnp.maximum(inten, 1.0)))
        x = quad(a * factor, c * factor, b * factor, d * factor).astype(BF16)
        a, b, c, d = blocks(both(mats[3], x, mats[2]))
        wr, wi = win[p, 0], win[p, 1]
        gphi[p] = quad(wr * a + wi * b, wr * c + wi * d, wr * b - wi * a, wr * d - wi * c).astype(BF16)
        pa, pb, pc, pd = blocks(phi[p])
        place(p, 0, pa * a + pb * b + pc * c + pd * d)
        place(p, 1, pa * b - pb * a + pc * d - pd * c)

    def fourth(p):
        a, b, c, d = blocks(both(mats[1], gphi[p], mats[0]))
        place(p, 0, probe[0, 0] * a + probe[0, 1] * b + probe[1, 0] * c + probe[1, 1] * d)
        place(p, 1, probe[0, 0] * b - probe[0, 1] * a + probe[1, 0] * d - probe[1, 1] * c)

    def scatter(s):
        for n in range(2 * THIRDS // 2):
            acc[s, :, n * T:(n + 1) * T] = dot(rows[...], parts[:, n * T:(n + 1) * T])

    def sums(s, q, k, start, size):
        n = THIRDS * q + k % THIRDS
        return acc[s, start:start + size, n * N:(n + 1) * N]

    def send_border(s):
        for n, (dr, dc) in enumerate(SIDES):
            start, size = {-1: (0, B), 0: (B, T), 1: (B + T, B)}[dr]
            if dc == 0:
                for q in range(2):
                    for j in range(2):
                        f0[n, s, q, j] = sums(s, q, 1 + j, start, size).astype(BF16)
            else:
                j = 0 if dc < 0 else 3
                x = pack(sums(s, 0, j, start, size), sums(s, 1, j, start, size), dc < 0)
                if n < 4:
                    f1[n - 2, s] = x
                else:
                    f2[n - 4, s] = x
        return [send(buffer_of((f0, f1, f2), n, s), buffer_of((g0, g1, g2), n, s), side) for n, side in enumerate(SIDES)]

    def add_border(s, copies):
        for q in range(2):
            for j in range(2):
                out[2 * s + q, :, j * N:(j + 1) * N] = sums(s, q, 1 + j, B, T)
        for n, (dr, dc) in enumerate(SIDES):
            copies[n].wait()
            there = exists((-dr, -dc))
            start, size = {-1: (T - B, B), 0: (0, T), 1: (0, B)}[dr]
            if dc == 0:
                for q in range(2):
                    for j in range(2):
                        out[2 * s + q, start:start + size, j * N:(j + 1) * N] += g0[n, s, q, j].astype(F32) * there
            else:
                j = 1 if dc < 0 else 0
                x = (g1[n - 2, s] if n < 4 else g2[n - 4, s]).astype(F32) * there
                lane = lanes(size)
                mine = (lane >= B) if dc < 0 else (lane < B)
                out[2 * s, start:start + size, j * N:(j + 1) * N] += jnp.where(mine, x, 0.0)
                out[2 * s + 1, start:start + size, j * N:(j + 1) * N] += jnp.where(mine, pltpu.roll(x, B, 1), 0.0)

    unpack_object(0)
    each(first)
    pass_on()
    unpack_object(1)
    each(second)
    end_amps()
    each(third)
    scatter(1)
    late = send_border(1)
    each(fourth)
    scatter(0)
    last = send_border(0)
    add_border(1, late)
    back = [fetch(9, out.at[pl.ds(2, 2)], out_h.at[pl.ds(2, 2)])]
    add_border(0, last)
    back.append(fetch(10, out.at[pl.ds(0, 2)], out_h.at[pl.ds(0, 2)]))
    for copy in back:
        copy.wait()


def local(objects, probe, amplitudes, owners, off_rows, off_cols):
    anywhere = pl.BlockSpec(memory_space=pl.ANY)
    vmem, smem = pltpu.VMEM, pltpu.SMEM
    i32 = jnp.int32
    gradient = pl.pallas_call(
        kernel,
        out_shape=jax.ShapeDtypeStruct((4, T, T), F32),
        in_specs=[anywhere] * 7,
        out_specs=anywhere,
        scratch_shapes=[
            vmem((4, T, T), F32), vmem((COUNT, N, N), BF16), *[smem((1, 1, COUNT), i32)] * 3,
            vmem((2, 2, N, N), F32), vmem((4, 2 * N, 2 * N), BF16), vmem((4, T, T), F32),
            vmem((4, CH, EXT, N), F32), *side_buffers(), *side_buffers(), *side_buffers(), *side_buffers(),
            vmem((KINDS, CAP, N, N), BF16), vmem((KINDS, CAP, N, N), BF16), vmem((CAP, N, N), BF16),
            vmem((KINDS, 8, N), i32), vmem((KINDS, 8, N), i32), smem((KINDS, 8, N), i32), smem((RMAX, 8), i32),
            vmem((RMAX, THIRDS, 8, N), F32), vmem((RMAX, 2 * N, 2 * N), F32), vmem((RMAX, 2 * N, 2 * N), F32),
            vmem((RMAX, 2, N, N), F32), vmem((RMAX, 2 * N, 2 * N), BF16),
            vmem((EXT, RMAX * N), BF16), vmem((RMAX * N, 2 * THIRDS * N), BF16), vmem((2, EXT, 2 * THIRDS * N), F32),
            pltpu.SemaphoreType.DMA((2, 4 * KINDS + 4 * len(SIDES))), pltpu.SemaphoreType.DMA((11,)),
        ],
        compiler_params=pltpu.CompilerParams(collective_id=0, has_side_effects=True, vmem_limit_bytes=56 << 20),
    )(objects.reshape(4, T, T), amplitudes.reshape(COUNT, N, N), owners, off_rows, off_cols, probe, tables())
    return gradient.reshape(objects.shape)


def solution(mesh):
    placed = (
        P(None, None, "row", "col"),
        P(),
        P("row", "col", None, None, None),
        P("row", "col", None),
        P("row", "col", None),
        P("row", "col", None),
    )
    return jax.shard_map(
        local, mesh=mesh, in_specs=placed, out_specs=P(None, None, "row", "col"), check_vma=False
    )
```

```python
import math

import jax
import jax.numpy as jnp
import numpy as np
from jax import lax
from jax.experimental import pallas as pl
from jax.experimental.pallas import tpu as pltpu
from jax.sharding import PartitionSpec as P

MESH = pl.DeviceIdType.MESH
REACH = (-3, -2, -1, 1, 2, 3, 4)
KINDS = len(REACH)
CAP = 2
SLOTS = CAP * KINDS
RMAX = 12
COUNT = 6
FRESNEL = 24.0
F32 = jnp.float32
BF16 = jnp.bfloat16
N = 128
B = 64
T = 256
EXT = T + 2 * B
CH = 4
SIDES = ((-1, 0), (1, 0), (0, -1), (0, 1), (-1, -1), (-1, 1), (1, -1), (1, 1))
XS = 8
PARTNERS = SIDES + tuple((0, d) for d in (-4, -3, -2, 2, 3, 4, -XS, XS))
THIRDS = 3
GROUP = 12


def tables():
    k = np.arange(N)
    f = np.exp(-2j * np.pi * ((k[:, None] * k[None, :]) % N) / N) / math.sqrt(N)
    c = (k + N // 2) % N - N // 2
    d = np.exp(-1j * np.pi * FRESNEL * c * c / (N * N))
    kk = np.conj(f) @ (d[:, None] * f)

    def left(a):
        return np.block([[a.real, -a.imag], [a.imag, a.real]]).astype(np.float32)

    return jnp.asarray(np.stack([left(kk), left(np.conj(kk)), left(f), left(np.conj(f))])).astype(BF16)


def at(side):
    nr, nc = lax.axis_size("row"), lax.axis_size("col")
    r, c = lax.axis_index("row"), lax.axis_index("col")
    return (lax.rem(r + side[0] + nr, nr), lax.rem(c + side[1] + nc, nc))


def exists(side):
    nr, nc = lax.axis_size("row"), lax.axis_size("col")
    r, c = lax.axis_index("row") + side[0], lax.axis_index("col") + side[1]
    inside = (r >= 0) & (r < nr) & (c >= 0) & (c < nc)
    return jnp.where(inside, 1.0, 0.0).astype(F32)


def lanes(rows):
    return lax.broadcasted_iota(jnp.int32, (rows, N), 1)


def pack(first, second, high):
    lane = lanes(first.shape[0])
    keep = (lane >= B) if high else (lane < B)
    return jnp.where(keep, first, pltpu.roll(second, B, 1)).astype(BF16)


def side_buffers():
    return [pltpu.VMEM((2, 2, 2, 2, B, N), BF16), pltpu.VMEM((2, 2, T, N), BF16), pltpu.VMEM((4, 2, B, N), BF16)]


def buffer_of(buffers, n, s):
    return buffers[0].at[n, s] if n < 2 else buffers[1].at[n - 2, s] if n < 4 else buffers[2].at[n - 4, s]


def dot(a, b):
    return jnp.dot(a, b, preferred_element_type=F32)


def blocks(x):
    return x[:N, :N], x[:N, N:], x[N:, :N], x[N:, N:]


def quad(a, b, c, d):
    return jnp.concatenate([jnp.concatenate([a, b], axis=1), jnp.concatenate([c, d], axis=1)], axis=0)


def both(left, x, right):
    a, b, c, d = blocks(dot(left, x).astype(BF16))
    return dot(quad(a, c, b, d), right)


def kernel(
    obj_h, amps_h, own_h, offr_h, offc_h, probe_h, mats_h, out_h,
    obj, amps, own, offr, offc, probe, mats, out,
    ext, s0, s1, s2, r0, r1, r2, f0, f1, f2, g0, g1, g2,
    s_amp, got_amp, passing, s_meta, got_meta, meta, plan, masks, phi, far, win, gphi, rows, parts, acc,
    sems, lsems,
):
    nc = lax.axis_size("col")
    me = lax.axis_index("col")
    used = [0]

    def prepare(src, dst, side, arrival=None):
        n = used[0]
        used[0] += 1
        return pltpu.make_async_remote_copy(
            src_ref=src, dst_ref=dst, send_sem=sems.at[0, n], recv_sem=sems.at[1, n if arrival is None else arrival],
            device_id=at(side), device_id_type=MESH,
        )

    def send(src, dst, side):
        copy = prepare(src, dst, side)
        copy.start()
        return copy

    barrier = pltpu.get_barrier_semaphore()
    for side in PARTNERS:
        pl.semaphore_signal(barrier, inc=1, device_id=at(side), device_id_type=MESH)

    def fetch(n, src, dst):
        copy = pltpu.make_async_copy(src, dst, lsems.at[n])
        copy.start()
        return copy

    in_ints = [fetch(n, a, b) for n, (a, b) in enumerate(((own_h, own), (offr_h, offr), (offc_h, offc)))]
    in_obj = [fetch(3 + s, obj_h.at[pl.ds(2 * s, 2)], obj.at[pl.ds(2 * s, 2)]) for s in range(2)]
    in_amps = fetch(5, amps_h, amps)
    in_probe, in_mats = fetch(6, probe_h, probe), fetch(7, mats_h, mats)

    def pack_object(s):
        for n, (dr, dc) in enumerate(SIDES):
            start, size = {-1: (0, B), 0: (0, T), 1: (T - B, B)}[dr]
            if dc == 0:
                for q in range(2):
                    for j in range(2):
                        s0[n, s, q, j] = obj[2 * s + q, start:start + size, j * N:(j + 1) * N].astype(BF16)
            else:
                j = 0 if dc < 0 else 1
                a = obj[2 * s, start:start + size, j * N:(j + 1) * N]
                b = obj[2 * s + 1, start:start + size, j * N:(j + 1) * N]
                if n < 4:
                    s1[n - 2, s] = pack(a, b, dc > 0)
                else:
                    s2[n - 4, s] = pack(a, b, dc > 0)

    in_obj[0].wait()
    pack_object(0)
    pl.semaphore_wait(barrier, len(PARTNERS))
    halo = [[send(buffer_of((s0, s1, s2), n, 0), buffer_of((r0, r1, r2), n, 0), side) for n, side in enumerate(SIDES)]]
    in_obj[1].wait()
    pack_object(1)
    halo.append([send(buffer_of((s0, s1, s2), n, 1), buffer_of((r0, r1, r2), n, 1), side) for n, side in enumerate(SIDES)])

    for copy in in_ints:
        copy.wait()
    dest = [own[0, 0, j] for j in range(COUNT)]
    apart = [lax.rem(d - me + nc, nc) for d in dest]
    rank = []
    for j in range(COUNT):
        same = jnp.int32(0)
        for i in range(j):
            same = same + jnp.where(dest[i] == dest[j], 1, 0)
        rank.append(same)
    chosen = []
    lane8 = lanes(8)
    for k, offset in enumerate(REACH):
        line = jnp.zeros((8, N), jnp.int32)
        for r in range(CAP):
            which, live, row, col = jnp.int32(0), jnp.int32(0), jnp.int32(0), jnp.int32(0)
            for j in range(COUNT):
                hit = (apart[j] == offset % nc) & (rank[j] == r)
                which = jnp.where(hit, j, which)
                live = jnp.where(hit, 1, live)
                row = jnp.where(hit, offr[0, 0, j], row)
                col = jnp.where(hit, offc[0, 0, j], col)
            chosen.append(which)
            for n, value in enumerate((live, row, col)):
                line = jnp.where(lane8 == 4 * r + n, value, line)
        s_meta[k] = line

    meta_copies = [send(s_meta.at[k], got_meta.at[k], (0, offset)) for k, offset in enumerate(REACH)]
    in_amps.wait()
    for k in range(KINDS):
        for r in range(CAP):
            s_amp[k, r] = amps[chosen[CAP * k + r]]

    x = lax.rem(me, XS)
    straight, detour, onward, turns = [], [], [], []
    for k, offset in enumerate(REACH):
        step = XS if offset > 0 else -XS
        turns.append(x == (XS - offset if offset > 0 else -1 - offset))
        arrival = used[0]
        straight.append(prepare(s_amp.at[k], got_amp.at[k], (0, offset)))
        detour.append(prepare(s_amp.at[k], passing, (0, step)))
        onward.append(prepare(passing, got_amp.at[k], (0, offset - step), arrival))

    def start_amps():
        for k in range(KINDS):
            @pl.when(turns[k])
            def _():
                detour[k].start()

            @pl.when(jnp.logical_not(turns[k]))
            def _():
                straight[k].start()

    def pass_on():
        for k in range(KINDS):
            @pl.when(turns[k])
            def _():
                detour[k].wait_recv()
                onward[k].start()

    def end_amps():
        for k in range(KINDS):
            straight[k].wait_recv()

            @pl.when(turns[k])
            def _():
                detour[k].wait_send()
                onward[k].wait_send()

            @pl.when(jnp.logical_not(turns[k]))
            def _():
                straight[k].wait_send()

    start_amps()

    for q in range(4):
        for j in range(2):
            ext[q, 1 + j, B:B + T] = obj[q, :, j * N:(j + 1) * N]

    in_probe.wait()
    in_mats.wait()
    for copy in meta_copies:
        copy.wait()
    to_smem = fetch(8, got_meta, meta)
    to_smem.wait()

    lives = [meta[i // CAP, 0, 4 * (i % CAP)] for i in range(SLOTS)]
    places, total = [], jnp.int32(0)
    for live in lives:
        places.append(total)
        total = total + live
    for p in range(RMAX):
        slot, live = jnp.int32(0), jnp.int32(0)
        for i in range(SLOTS):
            hit = (places[i] == p) & (lives[i] == 1)
            slot = jnp.where(hit, i, slot)
            live = jnp.where(hit, 1, live)
        kind, rank_in = slot // CAP, lax.rem(slot, CAP)
        row = meta[kind, 0, 4 * rank_in + 1] * live
        col = meta[kind, 0, 4 * rank_in + 2] * live + B
        base, shift = col // N, lax.rem(col, N)
        for n, value in enumerate((kind, rank_in, live, row, base, shift)):
            plan[p, n] = value
        for k in range(THIRDS):
            low = jnp.where(base == k, 1.0, 0.0).astype(F32)
            high = jnp.where((base + 1 == k) | (base + 1 == k + THIRDS), 1.0, 0.0).astype(F32)
            masks[p, k] = jnp.where(lane8 >= shift, low, high)
        away = lax.broadcasted_iota(jnp.int32, (EXT, N), 0) - lanes(EXT)
        rows[:, p * N:(p + 1) * N] = jnp.where(away == row, 1.0, 0.0).astype(BF16)

    def unpack_object(s):
        for n, (dr, dc) in enumerate(SIDES):
            halo[s][n].wait()
            there = exists((-dr, -dc))
            start, size = {-1: (B + T, B), 0: (B, T), 1: (0, B)}[dr]
            if dc == 0:
                for q in range(2):
                    for j in range(2):
                        ext[2 * s + q, 1 + j, start:start + size] = r0[n, s, q, j].astype(F32) * there
            else:
                j = 3 if dc < 0 else 0
                x = (r1[n - 2, s] if n < 4 else r2[n - 4, s]).astype(F32) * there
                ext[2 * s, j, start:start + size] = x
                ext[2 * s + 1, j, start:start + size] = pltpu.roll(x, B, 1)

    def window(q, p):
        row, base, shift = plan[p, 3], plan[p, 4], plan[p, 5]
        low = ext[q, base, pl.ds(row, N), :]
        high = ext[q, base + 1, pl.ds(row, N), :]
        return pltpu.roll(jnp.where(lanes(N) >= shift, low, high), N - shift, 1)

    def each(work):
        def step(n, carry):
            for i in range(GROUP):
                work(n * GROUP + i)
            return carry

        lax.fori_loop(0, RMAX // GROUP, step, 0)

    def first(p):
        wr, wi = window(0, p), window(1, p)
        psi = [(wr * probe[m, 0] - wi * probe[m, 1], wr * probe[m, 1] + wi * probe[m, 0]) for m in range(2)]
        x = quad(psi[0][0], psi[1][0], psi[0][1], psi[1][1]).astype(BF16)
        phi[p] = both(mats[0], x, mats[1])

    def second(p):
        wr, wi = window(2, p), window(3, p)
        win[p, 0], win[p, 1] = wr, wi
        a, b, c, d = blocks(phi[p])
        x = quad(a * wr - b * wi, c * wr - d * wi, a * wi + b * wr, c * wi + d * wr).astype(BF16)
        far[p] = both(mats[2], x, mats[3])

    def place(p, q, grad):
        t = pltpu.roll(grad, plan[p, 5], 1).reshape(N // 8, 8, N)
        for k in range(THIRDS):
            at_k = (t * masks[p, k]).reshape(N, N).astype(BF16)
            start = pl.multiple_of(p * N, N)
            parts[pl.ds(start, N), (THIRDS * q + k) * N:(THIRDS * q + k + 1) * N] = at_k

    def third(p):
        amp = got_amp[plan[p, 0], plan[p, 1]].astype(F32)
        live = plan[p, 2].astype(F32)
        a, b, c, d = blocks(far[p])
        inten = (a * a + b * b) + (c * c + d * d)
        factor = live * (1.0 - amp * lax.rsqrt(jnp.maximum(inten, 1.0)))
        x = quad(a * factor, c * factor, b * factor, d * factor).astype(BF16)
        a, b, c, d = blocks(both(mats[3], x, mats[2]))
        wr, wi = win[p, 0], win[p, 1]
        gphi[p] = quad(wr * a + wi * b, wr * c + wi * d, wr * b - wi * a, wr * d - wi * c).astype(BF16)
        pa, pb, pc, pd = blocks(phi[p])
        place(p, 0, pa * a + pb * b + pc * c + pd * d)
        place(p, 1, pa * b - pb * a + pc * d - pd * c)

    def fourth(p):
        a, b, c, d = blocks(both(mats[1], gphi[p], mats[0]))
        place(p, 0, probe[0, 0] * a + probe[0, 1] * b + probe[1, 0] * c + probe[1, 1] * d)
        place(p, 1, probe[0, 0] * b - probe[0, 1] * a + probe[1, 0] * d - probe[1, 1] * c)

    def scatter(s):
        for n in range(2 * THIRDS // 2):
            acc[s, :, n * T:(n + 1) * T] = dot(rows[...], parts[:, n * T:(n + 1) * T])

    def sums(s, q, k, start, size):
        n = THIRDS * q + k % THIRDS
        return acc[s, start:start + size, n * N:(n + 1) * N]

    def send_border(s):
        for n, (dr, dc) in enumerate(SIDES):
            start, size = {-1: (0, B), 0: (B, T), 1: (B + T, B)}[dr]
            if dc == 0:
                for q in range(2):
                    for j in range(2):
                        f0[n, s, q, j] = sums(s, q, 1 + j, start, size).astype(BF16)
            else:
                j = 0 if dc < 0 else 3
                x = pack(sums(s, 0, j, start, size), sums(s, 1, j, start, size), dc < 0)
                if n < 4:
                    f1[n - 2, s] = x
                else:
                    f2[n - 4, s] = x
        return [send(buffer_of((f0, f1, f2), n, s), buffer_of((g0, g1, g2), n, s), side) for n, side in enumerate(SIDES)]

    def add_border(s, copies):
        for q in range(2):
            for j in range(2):
                out[2 * s + q, :, j * N:(j + 1) * N] = sums(s, q, 1 + j, B, T)
        for n, (dr, dc) in enumerate(SIDES):
            copies[n].wait()
            there = exists((-dr, -dc))
            start, size = {-1: (T - B, B), 0: (0, T), 1: (0, B)}[dr]
            if dc == 0:
                for q in range(2):
                    for j in range(2):
                        out[2 * s + q, start:start + size, j * N:(j + 1) * N] += g0[n, s, q, j].astype(F32) * there
            else:
                j = 1 if dc < 0 else 0
                x = (g1[n - 2, s] if n < 4 else g2[n - 4, s]).astype(F32) * there
                lane = lanes(size)
                mine = (lane >= B) if dc < 0 else (lane < B)
                out[2 * s, start:start + size, j * N:(j + 1) * N] += jnp.where(mine, x, 0.0)
                out[2 * s + 1, start:start + size, j * N:(j + 1) * N] += jnp.where(mine, pltpu.roll(x, B, 1), 0.0)

    pass_on()
    unpack_object(0)
    each(first)
    unpack_object(1)
    each(second)
    end_amps()
    each(third)
    scatter(1)
    late = send_border(1)
    each(fourth)
    scatter(0)
    last = send_border(0)
    add_border(1, late)
    back = [fetch(9, out.at[pl.ds(2, 2)], out_h.at[pl.ds(2, 2)])]
    add_border(0, last)
    back.append(fetch(10, out.at[pl.ds(0, 2)], out_h.at[pl.ds(0, 2)]))
    for copy in back:
        copy.wait()


def local(objects, probe, amplitudes, owners, off_rows, off_cols):
    anywhere = pl.BlockSpec(memory_space=pl.ANY)
    vmem, smem = pltpu.VMEM, pltpu.SMEM
    i32 = jnp.int32
    gradient = pl.pallas_call(
        kernel,
        out_shape=jax.ShapeDtypeStruct((4, T, T), F32),
        in_specs=[anywhere] * 7,
        out_specs=anywhere,
        scratch_shapes=[
            vmem((4, T, T), F32), vmem((COUNT, N, N), BF16), *[smem((1, 1, COUNT), i32)] * 3,
            vmem((2, 2, N, N), F32), vmem((4, 2 * N, 2 * N), BF16), vmem((4, T, T), F32),
            vmem((4, CH, EXT, N), F32), *side_buffers(), *side_buffers(), *side_buffers(), *side_buffers(),
            vmem((KINDS, CAP, N, N), BF16), vmem((KINDS, CAP, N, N), BF16), vmem((CAP, N, N), BF16),
            vmem((KINDS, 8, N), i32), vmem((KINDS, 8, N), i32), smem((KINDS, 8, N), i32), smem((RMAX, 8), i32),
            vmem((RMAX, THIRDS, 8, N), F32), vmem((RMAX, 2 * N, 2 * N), F32), vmem((RMAX, 2 * N, 2 * N), F32),
            vmem((RMAX, 2, N, N), F32), vmem((RMAX, 2 * N, 2 * N), BF16),
            vmem((EXT, RMAX * N), BF16), vmem((RMAX * N, 2 * THIRDS * N), BF16), vmem((2, EXT, 2 * THIRDS * N), F32),
            pltpu.SemaphoreType.DMA((2, 4 * KINDS + 4 * len(SIDES))), pltpu.SemaphoreType.DMA((11,)),
        ],
        compiler_params=pltpu.CompilerParams(collective_id=0, has_side_effects=True, vmem_limit_bytes=56 << 20),
    )(objects.reshape(4, T, T), amplitudes.reshape(COUNT, N, N), owners, off_rows, off_cols, probe, tables())
    return gradient.reshape(objects.shape)


def solution(mesh):
    placed = (
        P(None, None, "row", "col"),
        P(),
        P("row", "col", None, None, None),
        P("row", "col", None),
        P("row", "col", None),
        P("row", "col", None),
    )
    return jax.shard_map(
        local, mesh=mesh, in_specs=placed, out_specs=P(None, None, "row", "col"), check_vma=False
    )
```

```python
import math

import jax
import jax.numpy as jnp
import numpy as np
from jax import lax
from jax.experimental import pallas as pl
from jax.experimental.pallas import tpu as pltpu
from jax.sharding import PartitionSpec as P

MESH = pl.DeviceIdType.MESH
REACH = (-3, -2, -1, 1, 2, 3, 4)
KINDS = len(REACH)
CAP = 2
SLOTS = CAP * KINDS
RMAX = 12
COUNT = 6
FRESNEL = 24.0
F32 = jnp.float32
BF16 = jnp.bfloat16
N = 128
B = 64
T = 256
EXT = T + 2 * B
CH = 4
SIDES = ((-1, 0), (1, 0), (0, -1), (0, 1), (-1, -1), (-1, 1), (1, -1), (1, 1))
XS = 8
PARTNERS = SIDES + tuple((0, d) for d in (-4, -3, -2, 2, 3, 4, -XS, XS))
THIRDS = 3
GROUP = 12


def tables():
    k = np.arange(N)
    f = np.exp(-2j * np.pi * ((k[:, None] * k[None, :]) % N) / N) / math.sqrt(N)
    c = (k + N // 2) % N - N // 2
    d = np.exp(-1j * np.pi * FRESNEL * c * c / (N * N))
    kk = np.conj(f) @ (d[:, None] * f)

    def left(a):
        return np.block([[a.real, -a.imag], [a.imag, a.real]]).astype(np.float32)

    return jnp.asarray(np.stack([left(kk), left(np.conj(kk)), left(f), left(np.conj(f))])).astype(BF16)


def at(side):
    nr, nc = lax.axis_size("row"), lax.axis_size("col")
    r, c = lax.axis_index("row"), lax.axis_index("col")
    return (lax.rem(r + side[0] + nr, nr), lax.rem(c + side[1] + nc, nc))


def exists(side):
    nr, nc = lax.axis_size("row"), lax.axis_size("col")
    r, c = lax.axis_index("row") + side[0], lax.axis_index("col") + side[1]
    inside = (r >= 0) & (r < nr) & (c >= 0) & (c < nc)
    return jnp.where(inside, 1.0, 0.0).astype(F32)


def lanes(rows):
    return lax.broadcasted_iota(jnp.int32, (rows, N), 1)


def pack(first, second, high):
    lane = lanes(first.shape[0])
    keep = (lane >= B) if high else (lane < B)
    return jnp.where(keep, first, pltpu.roll(second, B, 1)).astype(BF16)


def side_buffers():
    return [pltpu.VMEM((2, 2, 2, 2, B, N), BF16), pltpu.VMEM((2, 2, T, N), BF16), pltpu.VMEM((4, 2, B, N), BF16)]


def buffer_of(buffers, n, s):
    return buffers[0].at[n, s] if n < 2 else buffers[1].at[n - 2, s] if n < 4 else buffers[2].at[n - 4, s]


def dot(a, b):
    return jnp.dot(a, b, preferred_element_type=F32)


def blocks(x):
    return x[:N, :N], x[:N, N:], x[N:, :N], x[N:, N:]


def quad(a, b, c, d):
    return jnp.concatenate([jnp.concatenate([a, b], axis=1), jnp.concatenate([c, d], axis=1)], axis=0)


def both(left, x, right):
    a, b, c, d = blocks(dot(left, x).astype(BF16))
    return dot(quad(a, c, b, d), right)


def kernel(
    obj_h, amps_h, own_h, offr_h, offc_h, probe_h, mats_h, out_h,
    obj, amps, own, offr, offc, probe, mats, out,
    ext, s0, s1, s2, r0, r1, r2, f0, f1, f2, g0, g1, g2,
    s_amp, got_amp, passing, s_meta, got_meta, meta, plan, masks, phi, far, win, gphi, rows, parts, acc,
    sems, lsems,
):
    nc = lax.axis_size("col")
    me = lax.axis_index("col")
    used = [0]

    def prepare(src, dst, side, arrival=None):
        n = used[0]
        used[0] += 1
        return pltpu.make_async_remote_copy(
            src_ref=src, dst_ref=dst, send_sem=sems.at[0, n], recv_sem=sems.at[1, n if arrival is None else arrival],
            device_id=at(side), device_id_type=MESH,
        )

    def send(src, dst, side):
        copy = prepare(src, dst, side)
        copy.start()
        return copy

    barrier = pltpu.get_barrier_semaphore()
    for side in PARTNERS:
        pl.semaphore_signal(barrier, inc=1, device_id=at(side), device_id_type=MESH)

    def fetch(n, src, dst):
        copy = pltpu.make_async_copy(src, dst, lsems.at[n])
        copy.start()
        return copy

    in_ints = [fetch(n, a, b) for n, (a, b) in enumerate(((own_h, own), (offr_h, offr), (offc_h, offc)))]
    in_obj = [fetch(3 + s, obj_h.at[pl.ds(2 * s, 2)], obj.at[pl.ds(2 * s, 2)]) for s in range(2)]
    in_amps = fetch(5, amps_h, amps)
    in_probe, in_mats = fetch(6, probe_h, probe), fetch(7, mats_h, mats)

    def pack_object(s):
        for n, (dr, dc) in enumerate(SIDES):
            start, size = {-1: (0, B), 0: (0, T), 1: (T - B, B)}[dr]
            if dc == 0:
                for q in range(2):
                    for j in range(2):
                        s0[n, s, q, j] = obj[2 * s + q, start:start + size, j * N:(j + 1) * N].astype(BF16)
            else:
                j = 0 if dc < 0 else 1
                a = obj[2 * s, start:start + size, j * N:(j + 1) * N]
                b = obj[2 * s + 1, start:start + size, j * N:(j + 1) * N]
                if n < 4:
                    s1[n - 2, s] = pack(a, b, dc > 0)
                else:
                    s2[n - 4, s] = pack(a, b, dc > 0)

    in_obj[0].wait()
    pack_object(0)
    pl.semaphore_wait(barrier, len(PARTNERS))
    halo = [[send(buffer_of((s0, s1, s2), n, 0), buffer_of((r0, r1, r2), n, 0), side) for n, side in enumerate(SIDES)]]
    for copy in in_ints:
        copy.wait()
    dest = [own[0, 0, j] for j in range(COUNT)]
    apart = [lax.rem(d - me + nc, nc) for d in dest]
    rank = []
    for j in range(COUNT):
        same = jnp.int32(0)
        for i in range(j):
            same = same + jnp.where(dest[i] == dest[j], 1, 0)
        rank.append(same)
    chosen = []
    lane8 = lanes(8)
    for k, offset in enumerate(REACH):
        line = jnp.zeros((8, N), jnp.int32)
        for r in range(CAP):
            which, live, row, col = jnp.int32(0), jnp.int32(0), jnp.int32(0), jnp.int32(0)
            for j in range(COUNT):
                hit = (apart[j] == offset % nc) & (rank[j] == r)
                which = jnp.where(hit, j, which)
                live = jnp.where(hit, 1, live)
                row = jnp.where(hit, offr[0, 0, j], row)
                col = jnp.where(hit, offc[0, 0, j], col)
            chosen.append(which)
            for n, value in enumerate((live, row, col)):
                line = jnp.where(lane8 == 4 * r + n, value, line)
        s_meta[k] = line

    meta_copies = [send(s_meta.at[k], got_meta.at[k], (0, offset)) for k, offset in enumerate(REACH)]
    in_amps.wait()
    for k in range(KINDS):
        for r in range(CAP):
            s_amp[k, r] = amps[chosen[CAP * k + r]]

    x = lax.rem(me, XS)
    straight, detour, onward, turns = [], [], [], []
    for k, offset in enumerate(REACH):
        step = XS if offset > 0 else -XS
        turns.append(x == (XS - offset if offset > 0 else -1 - offset))
        arrival = used[0]
        straight.append(prepare(s_amp.at[k], got_amp.at[k], (0, offset)))
        detour.append(prepare(s_amp.at[k], passing, (0, step)))
        onward.append(prepare(passing, got_amp.at[k], (0, offset - step), arrival))

    def start_amps():
        for k in range(KINDS):
            @pl.when(turns[k])
            def _():
                detour[k].start()

            @pl.when(jnp.logical_not(turns[k]))
            def _():
                straight[k].start()

    def pass_on():
        for k in range(KINDS):
            @pl.when(turns[k])
            def _():
                detour[k].wait_recv()
                onward[k].start()

    def end_amps():
        for k in range(KINDS):
            straight[k].wait_recv()

            @pl.when(turns[k])
            def _():
                detour[k].wait_send()
                onward[k].wait_send()

            @pl.when(jnp.logical_not(turns[k]))
            def _():
                straight[k].wait_send()

    start_amps()
    in_obj[1].wait()
    pack_object(1)
    halo.append([send(buffer_of((s0, s1, s2), n, 1), buffer_of((r0, r1, r2), n, 1), side) for n, side in enumerate(SIDES)])

    for q in range(4):
        for j in range(2):
            ext[q, 1 + j, B:B + T] = obj[q, :, j * N:(j + 1) * N]

    in_probe.wait()
    in_mats.wait()
    for copy in meta_copies:
        copy.wait()
    to_smem = fetch(8, got_meta, meta)
    to_smem.wait()

    lives = [meta[i // CAP, 0, 4 * (i % CAP)] for i in range(SLOTS)]
    places, total = [], jnp.int32(0)
    for live in lives:
        places.append(total)
        total = total + live
    for p in range(RMAX):
        slot, live = jnp.int32(0), jnp.int32(0)
        for i in range(SLOTS):
            hit = (places[i] == p) & (lives[i] == 1)
            slot = jnp.where(hit, i, slot)
            live = jnp.where(hit, 1, live)
        kind, rank_in = slot // CAP, lax.rem(slot, CAP)
        row = meta[kind, 0, 4 * rank_in + 1] * live
        col = meta[kind, 0, 4 * rank_in + 2] * live + B
        base, shift = col // N, lax.rem(col, N)
        for n, value in enumerate((kind, rank_in, live, row, base, shift)):
            plan[p, n] = value
        for k in range(THIRDS):
            low = jnp.where(base == k, 1.0, 0.0).astype(F32)
            high = jnp.where((base + 1 == k) | (base + 1 == k + THIRDS), 1.0, 0.0).astype(F32)
            masks[p, k] = jnp.where(lane8 >= shift, low, high)
        away = lax.broadcasted_iota(jnp.int32, (EXT, N), 0) - lanes(EXT)
        rows[:, p * N:(p + 1) * N] = jnp.where(away == row, 1.0, 0.0).astype(BF16)

    def unpack_object(s):
        for n, (dr, dc) in enumerate(SIDES):
            halo[s][n].wait()
            there = exists((-dr, -dc))
            start, size = {-1: (B + T, B), 0: (B, T), 1: (0, B)}[dr]
            if dc == 0:
                for q in range(2):
                    for j in range(2):
                        ext[2 * s + q, 1 + j, start:start + size] = r0[n, s, q, j].astype(F32) * there
            else:
                j = 3 if dc < 0 else 0
                x = (r1[n - 2, s] if n < 4 else r2[n - 4, s]).astype(F32) * there
                ext[2 * s, j, start:start + size] = x
                ext[2 * s + 1, j, start:start + size] = pltpu.roll(x, B, 1)

    def window(q, p):
        row, base, shift = plan[p, 3], plan[p, 4], plan[p, 5]
        low = ext[q, base, pl.ds(row, N), :]
        high = ext[q, base + 1, pl.ds(row, N), :]
        return pltpu.roll(jnp.where(lanes(N) >= shift, low, high), N - shift, 1)

    def each(work):
        def step(n, carry):
            for i in range(GROUP):
                work(n * GROUP + i)
            return carry

        lax.fori_loop(0, RMAX // GROUP, step, 0)

    def first(p):
        wr, wi = window(0, p), window(1, p)
        psi = [(wr * probe[m, 0] - wi * probe[m, 1], wr * probe[m, 1] + wi * probe[m, 0]) for m in range(2)]
        x = quad(psi[0][0], psi[1][0], psi[0][1], psi[1][1]).astype(BF16)
        phi[p] = both(mats[0], x, mats[1])

    def second(p):
        wr, wi = window(2, p), window(3, p)
        win[p, 0], win[p, 1] = wr, wi
        a, b, c, d = blocks(phi[p])
        x = quad(a * wr - b * wi, c * wr - d * wi, a * wi + b * wr, c * wi + d * wr).astype(BF16)
        far[p] = both(mats[2], x, mats[3])

    def place(p, q, grad):
        t = pltpu.roll(grad, plan[p, 5], 1).reshape(N // 8, 8, N)
        for k in range(THIRDS):
            at_k = (t * masks[p, k]).reshape(N, N).astype(BF16)
            start = pl.multiple_of(p * N, N)
            parts[pl.ds(start, N), (THIRDS * q + k) * N:(THIRDS * q + k + 1) * N] = at_k

    def third(p):
        amp = got_amp[plan[p, 0], plan[p, 1]].astype(F32)
        live = plan[p, 2].astype(F32)
        a, b, c, d = blocks(far[p])
        inten = (a * a + b * b) + (c * c + d * d)
        factor = live * (1.0 - amp * lax.rsqrt(jnp.maximum(inten, 1.0)))
        x = quad(a * factor, c * factor, b * factor, d * factor).astype(BF16)
        a, b, c, d = blocks(both(mats[3], x, mats[2]))
        wr, wi = win[p, 0], win[p, 1]
        gphi[p] = quad(wr * a + wi * b, wr * c + wi * d, wr * b - wi * a, wr * d - wi * c).astype(BF16)
        pa, pb, pc, pd = blocks(phi[p])
        place(p, 0, pa * a + pb * b + pc * c + pd * d)
        place(p, 1, pa * b - pb * a + pc * d - pd * c)

    def fourth(p):
        a, b, c, d = blocks(both(mats[1], gphi[p], mats[0]))
        place(p, 0, probe[0, 0] * a + probe[0, 1] * b + probe[1, 0] * c + probe[1, 1] * d)
        place(p, 1, probe[0, 0] * b - probe[0, 1] * a + probe[1, 0] * d - probe[1, 1] * c)

    def scatter(s):
        for n in range(2 * THIRDS // 2):
            acc[s, :, n * T:(n + 1) * T] = dot(rows[...], parts[:, n * T:(n + 1) * T])

    def sums(s, q, k, start, size):
        n = THIRDS * q + k % THIRDS
        return acc[s, start:start + size, n * N:(n + 1) * N]

    def send_border(s):
        for n, (dr, dc) in enumerate(SIDES):
            start, size = {-1: (0, B), 0: (B, T), 1: (B + T, B)}[dr]
            if dc == 0:
                for q in range(2):
                    for j in range(2):
                        f0[n, s, q, j] = sums(s, q, 1 + j, start, size).astype(BF16)
            else:
                j = 0 if dc < 0 else 3
                x = pack(sums(s, 0, j, start, size), sums(s, 1, j, start, size), dc < 0)
                if n < 4:
                    f1[n - 2, s] = x
                else:
                    f2[n - 4, s] = x
        return [send(buffer_of((f0, f1, f2), n, s), buffer_of((g0, g1, g2), n, s), side) for n, side in enumerate(SIDES)]

    def add_border(s, copies):
        for q in range(2):
            for j in range(2):
                out[2 * s + q, :, j * N:(j + 1) * N] = sums(s, q, 1 + j, B, T)
        for n, (dr, dc) in enumerate(SIDES):
            copies[n].wait()
            there = exists((-dr, -dc))
            start, size = {-1: (T - B, B), 0: (0, T), 1: (0, B)}[dr]
            if dc == 0:
                for q in range(2):
                    for j in range(2):
                        out[2 * s + q, start:start + size, j * N:(j + 1) * N] += g0[n, s, q, j].astype(F32) * there
            else:
                j = 1 if dc < 0 else 0
                x = (g1[n - 2, s] if n < 4 else g2[n - 4, s]).astype(F32) * there
                lane = lanes(size)
                mine = (lane >= B) if dc < 0 else (lane < B)
                out[2 * s, start:start + size, j * N:(j + 1) * N] += jnp.where(mine, x, 0.0)
                out[2 * s + 1, start:start + size, j * N:(j + 1) * N] += jnp.where(mine, pltpu.roll(x, B, 1), 0.0)

    pass_on()
    unpack_object(0)
    each(first)
    unpack_object(1)
    each(second)
    end_amps()
    each(third)
    scatter(1)
    late = send_border(1)
    each(fourth)
    scatter(0)
    last = send_border(0)
    add_border(1, late)
    back = [fetch(9, out.at[pl.ds(2, 2)], out_h.at[pl.ds(2, 2)])]
    add_border(0, last)
    back.append(fetch(10, out.at[pl.ds(0, 2)], out_h.at[pl.ds(0, 2)]))
    for copy in back:
        copy.wait()


def local(objects, probe, amplitudes, owners, off_rows, off_cols):
    anywhere = pl.BlockSpec(memory_space=pl.ANY)
    vmem, smem = pltpu.VMEM, pltpu.SMEM
    i32 = jnp.int32
    gradient = pl.pallas_call(
        kernel,
        out_shape=jax.ShapeDtypeStruct((4, T, T), F32),
        in_specs=[anywhere] * 7,
        out_specs=anywhere,
        scratch_shapes=[
            vmem((4, T, T), F32), vmem((COUNT, N, N), BF16), *[smem((1, 1, COUNT), i32)] * 3,
            vmem((2, 2, N, N), F32), vmem((4, 2 * N, 2 * N), BF16), vmem((4, T, T), F32),
            vmem((4, CH, EXT, N), F32), *side_buffers(), *side_buffers(), *side_buffers(), *side_buffers(),
            vmem((KINDS, CAP, N, N), BF16), vmem((KINDS, CAP, N, N), BF16), vmem((CAP, N, N), BF16),
            vmem((KINDS, 8, N), i32), vmem((KINDS, 8, N), i32), smem((KINDS, 8, N), i32), smem((RMAX, 8), i32),
            vmem((RMAX, THIRDS, 8, N), F32), vmem((RMAX, 2 * N, 2 * N), F32), vmem((RMAX, 2 * N, 2 * N), F32),
            vmem((RMAX, 2, N, N), F32), vmem((RMAX, 2 * N, 2 * N), BF16),
            vmem((EXT, RMAX * N), BF16), vmem((RMAX * N, 2 * THIRDS * N), BF16), vmem((2, EXT, 2 * THIRDS * N), F32),
            pltpu.SemaphoreType.DMA((2, 4 * KINDS + 4 * len(SIDES))), pltpu.SemaphoreType.DMA((11,)),
        ],
        compiler_params=pltpu.CompilerParams(collective_id=0, has_side_effects=True, vmem_limit_bytes=56 << 20),
    )(objects.reshape(4, T, T), amplitudes.reshape(COUNT, N, N), owners, off_rows, off_cols, probe, tables())
    return gradient.reshape(objects.shape)


def solution(mesh):
    placed = (
        P(None, None, "row", "col"),
        P(),
        P("row", "col", None, None, None),
        P("row", "col", None),
        P("row", "col", None),
        P("row", "col", None),
    )
    return jax.shard_map(
        local, mesh=mesh, in_specs=placed, out_specs=P(None, None, "row", "col"), check_vma=False
    )
```
